256 devices in a mesh: gx: 16 (over x_lo, z), gy: 4 (over y), gz: 4 (over x_hi, core).
Axes of the slice: x: 4 (x_hi: 2, x_lo: 2; x = x_hi * 2 + x_lo), y: 4, z: 8, core: 2. Of those that a mesh axis runs over, the one named last changes fastest.
Arguments:
- coeffs: float32 [2, 64, 524288], P(None, None, ('gx', 'gy', 'gz')), may hold values from -6 to 6
- interp: float32 [3, 3, 2, 2, 64, 64], replicated, may hold values from -0.375 to 0.375
- freq_index: int32 [3, 3, 2, 64], replicated, may hold values from 1 to 1023
- target: int32 [524288], P(('gx', 'gy', 'gz')), may hold values from 0 to 1023
Outputs:
- projected: float32 [2, 64, 524288], P(None, None, ('gx', 'gy', 'gz'))
The draws below stay inside these ranges and needn't reach their ends.
All inputs are finite; a program needn't handle non-finite values.
Results may differ from the reference program's by a relative error of at most 0.0001.
Values sent between devices are 32-bit elements; how exact they have to be, the bound alone decides.
A program may use at most 64 MiB of HBM per device.

```python
import math
import jax
import jax.numpy as jnp
from jax import lax

PTS = 64
LEVELS = 3
BOX_DEV = 2048
BOXES = 524288
N_GX = 16
N_GY = 4
N_GZ = 4


def with_ends(entries, key, smallest, high):
    place = [jax.random.randint(jax.random.fold_in(key, axis), (), 0, length) for axis, length in enumerate(entries.shape)]
    widest = entries.shape.index(max(entries.shape))
    beside = place[:widest] + [(place[widest] + 1) % entries.shape[widest]] + place[widest + 1:]
    return entries.at[tuple(place)].set(smallest).at[tuple(beside)].set(high)


def block_scale(own_key, dims, cuts, least, top_value):
    factor_of, own = 1.0, jax.random.fold_in(own_key, 6)
    for axis_at, shards_of in cuts:
        draws = jnp.exp(jax.random.uniform(jax.random.fold_in(own, axis_at), (shards_of,), jnp.float32, least / len(cuts), top_value / len(cuts)))
        factor_of = factor_of * jnp.repeat(draws, dims[axis_at] // shards_of).reshape([-1 if axis == axis_at else 1 for axis in range(len(dims))])
    return factor_of


def scatter_about(rng, shape, scale, reach, cuts=(), kind=jnp.bfloat16):
    entries = jax.random.normal(rng, shape, jnp.float32) * scale
    if len(cuts) > 0:
        entries = block_scale(rng, shape, cuts, -0.22, 0.18) * entries
    return jnp.clip(entries, min=-reach, max=reach).astype(kind)


def setup_inputs(seed: int = 0) -> dict:
    splits = jax.random.split(jax.random.key(seed), 5)
    return {
        "coeffs": scatter_about(splits[0], (2, PTS, BOXES), 1.0, 6.0, ((2, 256),), jnp.float32),
        "interp": scatter_about(splits[1], (LEVELS, 3, 2, 2, PTS, PTS), (4 * PTS) ** -0.5, 0.375, (), jnp.float32),
        "freq_index": with_ends(jax.random.randint(splits[2], (LEVELS, 3, 2, PTS), 1, 1024), jax.random.fold_in(splits[2], 1), 1, 1023).astype(jnp.int32),
        "target": with_ends(jax.random.randint(splits[3], (BOXES,), 0, 1024), jax.random.fold_in(splits[3], 1), 0, 1023).astype(jnp.int32),
    }


def flip_bit(values, dim, bit):
    shape = values.shape
    count = shape[dim]
    parted = values.reshape(shape[:dim] + (count >> (bit + 1), 2, 1 << bit) + shape[dim + 1:])
    return jnp.flip(parted, dim + 1).reshape(shape)


def complex_apply(mats, rot_re, rot_im):
    highest = lax.Precision.HIGHEST
    new_re = jnp.zeros(rot_re.shape[1:], jnp.float32)
    new_im = jnp.zeros(rot_re.shape[1:], jnp.float32)
    for child in range(2):
        real_part = mats[child, 0]
        imag_part = mats[child, 1]
        new_re = new_re + jnp.dot(real_part, rot_re[child], precision=highest, preferred_element_type=jnp.float32) - jnp.dot(imag_part, rot_im[child], precision=highest, preferred_element_type=jnp.float32)
        new_im = new_im + jnp.dot(imag_part, rot_re[child], precision=highest, preferred_element_type=jnp.float32) + jnp.dot(real_part, rot_im[child], precision=highest, preferred_element_type=jnp.float32)
    return new_re, new_im


def reference(coeffs, interp, freq_index, target):
    counts = (N_GX, N_GY, N_GZ)
    state = coeffs.reshape(2, PTS, N_GX, N_GY, N_GZ, BOX_DEV)
    grid = target.reshape(N_GX, N_GY, N_GZ, BOX_DEV)
    for level in range(LEVELS):
        for step in range(3):
            count = counts[step]
            nbits = count.bit_length() - 1
            if step == 0:
                bit = (nbits - 1 - level) % nbits
            else:
                bit = level % nbits
            other = flip_bit(state, 2 + step, bit)
            shape = [1, 1, 1, 1, 1, 1]
            shape[2 + step] = count
            side = ((jnp.arange(count, dtype=jnp.int32) >> bit) & 1).reshape(shape)
            lower = jnp.where(side == 0, state, other)
            upper = jnp.where(side == 0, other, state)
            kidx = freq_index[level, step]
            phase_idx = (grid[None, None] * kidx[:, :, None, None, None, None]) % 1024
            angle = phase_idx.astype(jnp.float32) * (2.0 * math.pi / 1024.0)
            cosv = jnp.cos(angle)
            sinv = jnp.sin(angle)
            members = jnp.stack([lower, upper])
            rot_re = cosv * members[:, 0] - sinv * members[:, 1]
            rot_im = sinv * members[:, 0] + cosv * members[:, 1]
            rot_re = rot_re.reshape(2, PTS, -1)
            rot_im = rot_im.reshape(2, PTS, -1)
            new_re, new_im = complex_apply(interp[level, step], rot_re, rot_im)
            state = jnp.stack([new_re, new_im]).reshape(state.shape)
    return state.reshape(2, PTS, -1)
```

```python
import functools
import math

import jax
import jax.numpy as jnp
import numpy as np
from jax import lax
from jax.experimental import pallas as pl
from jax.experimental.pallas import tpu as pltpu
from jax.sharding import PartitionSpec as P

MESH = pl.DeviceIdType.MESH
GROUP = 128
PEERS = GROUP - 1
CHUNKS = 2
ROWS = 8
CHUNK = GROUP * ROWS
STEP_BITS = (6, 2, 0, 5, 3, 1, 4, 2, 0)
BLOCK = 256


def turn_cos_coefficients(degree=6):
    nodes = np.cos((np.arange(400) + 0.5) * np.pi / 400)
    z = (nodes + 1) / 8
    cheb = np.polynomial.chebyshev.Chebyshev.fit(
        z, np.cos(2 * np.pi * np.sqrt(z)), degree, domain=[0, 0.25]
    )
    poly = cheb.convert(kind=np.polynomial.Polynomial, domain=[-1, 1], window=[-1, 1])
    return [float(c) for c in poly.coef]


COS = turn_cos_coefficients()


def turn_cos(r):
    x = r - jnp.round(r)
    z = x * x
    acc = jnp.full_like(z, COS[-1])
    for c in COS[-2::-1]:
        acc = acc * z + c
    return acc


def place():
    gx, gy, gz = lax.axis_index("gx"), lax.axis_index("gy"), lax.axis_index("gz")
    return gx // 8, (gx // 2) % 4, gy, gz, gx % 2


def number(xlo, z, y, g):
    return ((xlo * 4 + z) * 4 + y) * 4 + g


def each_peer(fn):
    xlo, z, y, g, low = place()

    def visit(dz, i):
        px = (xlo + i // 16) % 2
        pz = (z + dz) % 4
        py = (y + (i // 4) % 4) % 4
        pg = (g + i % 4) % 4
        fn((px * 8 + pz * 2 + low, py, pg), number(px, pz, py, pg))

    for dz in (2, 1, 3, 0):

        def body(i, carry, dz=dz):
            visit(dz, i)
            return carry

        lax.fori_loop(1 if dz == 0 else 0, 32, body, 0)


def kernel(
    coeffs_ref, interp_ref, freq_ref, target_ref, out_ref,
    x_ref, send0, send1, recv0, recv1, state, back0, back1, final0, final1, y_ref,
    tsend, trecv, turns, freqs, wide, weights, phase,
    load_sem, store_sem, tsend_sem, trecv_sem, in_send, in_recv, out_send, out_recv,
):
    xlo, z, y, g, low = place()
    me = number(xlo, z, y, g)
    send, recv, back, final = (send0, send1), (recv0, recv1), (back0, back1), (final0, final1)
    half = CHUNK

    def load(q):
        cols = pl.ds(q * half, half)
        return pltpu.make_async_copy(
            coeffs_ref.at[:, :, cols], x_ref.at[:, :, cols], load_sem.at[q]
        )

    for q in range(CHUNKS):
        load(q).start()
    barrier = pltpu.get_barrier_semaphore()
    each_peer(
        lambda device, d: pl.semaphore_signal(
            barrier, inc=1, device_id=device, device_id_type=MESH
        )
    )

    targets = target_ref[...].astype(jnp.float32)
    for k in range(8):
        for q in range(CHUNKS):
            tsend[k, q : q + 1, :] = targets[q * 8 + k : q * 8 + k + 1, :]

    def turn_in(q):
        load(q).wait()
        for j in range(half // 128):
            cols = slice(q * half + j * 128, q * half + (j + 1) * 128)
            block = x_ref[:, :, cols].reshape(128, 128)
            send[q][j * 128 : (j + 1) * 128, :] = block.T

    def copy_in(q, device, d):
        return pltpu.make_async_remote_copy(
            src_ref=send[q].at[pl.ds(pl.multiple_of(d * ROWS, ROWS), ROWS)],
            dst_ref=recv[q].at[pl.ds(pl.multiple_of(me * ROWS, ROWS), ROWS)],
            send_sem=in_send.at[q],
            recv_sem=in_recv.at[q],
            device_id=device,
            device_id_type=MESH,
        )

    def copy_out(q, device, d):
        return pltpu.make_async_remote_copy(
            src_ref=back[q].at[pl.ds(pl.multiple_of(d * ROWS, ROWS), ROWS)],
            dst_ref=final[q].at[pl.ds(pl.multiple_of(me * ROWS, ROWS), ROWS)],
            send_sem=out_send.at[q],
            recv_sem=out_recv.at[q],
            device_id=device,
            device_id_type=MESH,
        )

    def copy_target(device, d):
        return pltpu.make_async_remote_copy(
            src_ref=tsend.at[d // 16],
            dst_ref=trecv.at[me],
            send_sem=tsend_sem,
            recv_sem=trecv_sem,
            device_id=device,
            device_id_type=MESH,
        )

    def all_of(ref, sem):
        part = ref.at[pl.ds(0, PEERS * ROWS)]
        return pltpu.make_async_copy(part, part, sem)

    def all_targets(sem):
        part = trecv.at[pl.ds(0, PEERS)]
        return pltpu.make_async_copy(part, part, sem)

    turn_in(0)
    pl.semaphore_wait(barrier, PEERS)
    each_peer(lambda device, d: copy_target(device, d).start())
    each_peer(lambda device, d: copy_in(0, device, d).start())
    turn_in(1)
    each_peer(lambda device, d: copy_in(1, device, d).start())
    own = pl.ds(pl.multiple_of(me * ROWS, ROWS), ROWS)
    for q in range(CHUNKS):
        recv[q][own, :] = send[q][own, :]
    trecv[me] = tsend[me // 16]

    for k in range(9):
        level, s = divmod(k, 3)
        for c in range(2):
            re = interp_ref[level, s, c, 0]
            im = interp_ref[level, s, c, 1]
            wide[0:64, 0:64] = re
            wide[0:64, 64:128] = -im
            wide[64:128, 0:64] = im
            wide[64:128, 64:128] = re
            w = wide[...].T
            hi = w.astype(jnp.bfloat16)
            lo = (w - hi.astype(jnp.float32)).astype(jnp.bfloat16)
            rows = slice(c * 128, (c + 1) * 128)
            weights[k, rows, 0:128] = hi
            weights[k, rows, 128:256] = lo
    for level in range(3):
        for s in range(3):
            f = freq_ref[level, s].astype(jnp.float32) * (1.0 / 1024.0)
            k = (level * 3 + s) * 2
            freqs[k : k + 2, 0:64] = f
            freqs[k : k + 2, 64:128] = f

    lane = lax.broadcasted_iota(jnp.int32, (8, 128), 1)
    row = lax.broadcasted_iota(jnp.int32, (8, 128), 0)
    mine = lane == (me % 16) * ROWS + row
    all_targets(trecv_sem).wait()
    for q in range(CHUNKS):

        def gather(i, carry, q=q):
            t = trecv[i, q : q + 1, :]
            t = jnp.sum(jnp.where(mine, t, 0.0), axis=1, keepdims=True)
            turns[pl.ds(pl.multiple_of(q * half + i * 8, 8), 8), :] = jnp.broadcast_to(t, (8, 128))
            return carry

        lax.fori_loop(0, GROUP, gather, 0, unroll=8)

    quarter = jnp.where(lax.broadcasted_iota(jnp.int32, (1, 128), 1) < 64, 0.0, -0.25)
    for q in range(CHUNKS):

        def fill(i, carry, q=q):
            rows = pl.ds(pl.multiple_of(q * half + i * 64, 64), 64)
            t = turns[rows, :]
            for k in range(18):
                phase[k, rows, :] = turn_cos(t * freqs[k : k + 1, :] + quarter)
            return carry

        lax.fori_loop(0, half // 64, fill, 0)

    def rotate(p, x, swapped, low_half):
        other = pltpu.roll(p, 64, 1)
        c = jnp.where(low_half, p, other)
        s = jnp.where(low_half, other, p)
        return c * x + s * swapped

    def mix(k, base, lo_rows, child0, child1):
        rows = pl.ds(pl.multiple_of(base + lo_rows, 8), child0.shape[0])
        low_half = lax.broadcasted_iota(jnp.int32, child0.shape, 1) < 64
        sign = jnp.where(low_half, -1.0, 1.0)
        rot = []
        for c, x in enumerate((child0, child1)):
            swapped = pltpu.roll(x, 64, 1) * sign
            rot.append(rotate(phase[2 * k + c, rows, :], x, swapped, low_half))
        rot = jnp.concatenate(rot, axis=1)
        hi = rot.astype(jnp.bfloat16)
        lo = (rot - hi.astype(jnp.float32)).astype(jnp.bfloat16)
        both = jnp.dot(hi, weights[k], preferred_element_type=jnp.float32)
        rest = jnp.dot(lo, weights[k, :, 0:128], preferred_element_type=jnp.float32)
        return both[:, 0:128] + both[:, 128:256] + rest

    def step(k, q, src, dst):
        stride = ROWS << STEP_BITS[k]
        base = q * half
        part = BLOCK // 2

        def body(b, carry):
            if stride >= part:
                per = stride // part
                at = (b // per) * (2 * stride) + (b % per) * part
                x0 = src[pl.ds(pl.multiple_of(at, part), part), :]
                x1 = src[pl.ds(pl.multiple_of(at + stride, part), part), :]
                new0 = mix(k, base, at, x0, x1)
                new1 = mix(k, base, at + stride, x0, x1)
                dst[pl.ds(pl.multiple_of(at, part), part), :] = new0
                dst[pl.ds(pl.multiple_of(at + stride, part), part), :] = new1
            else:
                rows = pl.ds(pl.multiple_of(b * BLOCK, BLOCK), BLOCK)
                x = src[rows, :].reshape(BLOCK // (2 * stride), 2, stride, 128)
                children = [
                    jnp.broadcast_to(x[:, c : c + 1], x.shape).reshape(BLOCK, 128) for c in range(2)
                ]
                dst[rows, :] = mix(k, base, b * BLOCK, *children)
            return carry

        lax.fori_loop(0, half // BLOCK, body, 0)

    for q in range(CHUNKS):
        all_of(recv[q], in_recv.at[q]).wait()
        for k in range(9):
            step(k, q, recv[q] if k == 0 else state, back[q] if k == 8 else state)
        each_peer(lambda device, d, q=q: copy_out(q, device, d).start())
        final[q][own, :] = back[q][own, :]

    def store(q):
        cols = pl.ds(q * half, half)
        return pltpu.make_async_copy(
            y_ref.at[:, :, cols], out_ref.at[:, :, cols], store_sem.at[q]
        )

    for q in range(CHUNKS):
        all_of(final[q], out_recv.at[q]).wait()
        for j in range(half // 128):
            block = final[q][j * 128 : (j + 1) * 128, :]
            cols = slice(q * half + j * 128, q * half + (j + 1) * 128)
            y_ref[:, :, cols] = block.T.reshape(2, 64, 128)
        store(q).start()
    all_targets(tsend_sem).wait()
    for q in range(CHUNKS):
        all_of(send[q], in_send.at[q]).wait()
        all_of(back[q], out_send.at[q]).wait()
        store(q).wait()


def shards(coeffs, interp, freq_index, target):
    f32 = jnp.float32
    anywhere = pl.BlockSpec(memory_space=pl.ANY)
    vmem = pl.BlockSpec(memory_space=pltpu.VMEM)
    big = pltpu.VMEM((CHUNK, 128), f32)
    dma = pltpu.SemaphoreType.DMA
    return pl.pallas_call(
        kernel,
        out_shape=jax.ShapeDtypeStruct(coeffs.shape, f32),
        in_specs=[anywhere, vmem, vmem, vmem],
        out_specs=anywhere,
        scratch_shapes=[
            pltpu.VMEM(coeffs.shape, f32),
            big, big, big, big, big, big, big, big, big,
            pltpu.VMEM(coeffs.shape, f32),
            pltpu.VMEM((8, CHUNKS, 128), f32),
            pltpu.VMEM((GROUP, CHUNKS, 128), f32),
            pltpu.VMEM((CHUNKS * CHUNK, 128), f32),
            pltpu.VMEM((24, 128), f32),
            pltpu.VMEM((128, 128), f32),
            pltpu.VMEM((9, 256, 256), jnp.bfloat16),
            pltpu.VMEM((18, CHUNKS * CHUNK, 128), f32),
            dma((CHUNKS,)), dma((CHUNKS,)), dma, dma,
            dma((CHUNKS,)), dma((CHUNKS,)), dma((CHUNKS,)), dma((CHUNKS,)),
        ],
        compiler_params=pltpu.CompilerParams(
            collective_id=0, has_side_effects=True, vmem_limit_bytes=60 * 1024 * 1024
        ),
        name="butterfly",
    )(coeffs, interp, freq_index, target.reshape(16, 128))


def solution(mesh):
    in_specs = (P(None, None, ("gx", "gy", "gz")), P(), P(), P(("gx", "gy", "gz")))
    out_specs = P(None, None, ("gx", "gy", "gz"))
    return jax.shard_map(shards, mesh=mesh, in_specs=in_specs, out_specs=out_specs, check_vma=False)
```

```python
import functools
import math

import jax
import jax.numpy as jnp
import numpy as np
from jax import lax
from jax.experimental import pallas as pl
from jax.experimental.pallas import tpu as pltpu
from jax.sharding import PartitionSpec as P

MESH = pl.DeviceIdType.MESH
GROUP = 128
PEERS = GROUP - 1
CHUNKS = 2
ROWS = 8
CHUNK = GROUP * ROWS
STEP_BITS = (6, 2, 0, 5, 3, 1, 4, 2, 0)
BLOCK = 256


def turn_cos_coefficients(degree=6):
    nodes = np.cos((np.arange(400) + 0.5) * np.pi / 400)
    z = (nodes + 1) / 8
    cheb = np.polynomial.chebyshev.Chebyshev.fit(
        z, np.cos(2 * np.pi * np.sqrt(z)), degree, domain=[0, 0.25]
    )
    poly = cheb.convert(kind=np.polynomial.Polynomial, domain=[-1, 1], window=[-1, 1])
    return [float(c) for c in poly.coef]


COS = turn_cos_coefficients()


def turn_cos(r):
    x = r - jnp.round(r)
    z = x * x
    acc = jnp.full_like(z, COS[-1])
    for c in COS[-2::-1]:
        acc = acc * z + c
    return acc


def place():
    gx, gy, gz = lax.axis_index("gx"), lax.axis_index("gy"), lax.axis_index("gz")
    return gx // 8, (gx // 2) % 4, gy, gz, gx % 2


def number(xlo, z, y, g):
    return ((xlo * 4 + z) * 4 + y) * 4 + g


def each_peer(fn):
    xlo, z, y, g, low = place()
    xs = [(xlo + i) % 2 for i in range(2)]
    zs = [(z + i) % 4 for i in range(4)]
    ys = [(y + i) % 4 for i in range(4)]
    gs = [(g + i) % 4 for i in range(4)]
    for dz in (2, 1, 3, 0):
        for dx in range(2):
            gx = xs[dx] * 8 + zs[dz] * 2 + low
            first = number(xs[dx], zs[dz], 0, 0)
            for dy in range(4):
                for dg in range(4):
                    if dz or dx or dy or dg:
                        fn((gx, ys[dy], gs[dg]), first + ys[dy] * 4 + gs[dg])


def kernel(
    coeffs_ref, interp_ref, freq_ref, target_ref, out_ref,
    x_ref, send0, send1, recv0, recv1, state0, state1, back0, back1, final0, final1, y_ref,
    tsend, trecv, turns, freqs, wide, weights, cosines, sines,
    load_sem, store_sem, tsend_sem, trecv_sem, in_send, in_recv, out_send, out_recv,
):
    xlo, z, y, g, low = place()
    me = number(xlo, z, y, g)
    send, recv, back, final = (send0, send1), (recv0, recv1), (back0, back1), (final0, final1)
    half = CHUNK

    def load(q):
        cols = pl.ds(q * half, half)
        return pltpu.make_async_copy(
            coeffs_ref.at[:, :, cols], x_ref.at[:, :, cols], load_sem.at[q]
        )

    for q in range(CHUNKS):
        load(q).start()
    barrier = pltpu.get_barrier_semaphore()
    each_peer(
        lambda device, d: pl.semaphore_signal(
            barrier, inc=1, device_id=device, device_id_type=MESH
        )
    )

    targets = target_ref[...].astype(jnp.float32)
    for k in range(8):
        for q in range(CHUNKS):
            tsend[k, q : q + 1, :] = targets[q * 8 + k : q * 8 + k + 1, :]

    def turn_in(q):
        load(q).wait()
        for j in range(half // 128):
            cols = slice(q * half + j * 128, q * half + (j + 1) * 128)
            block = x_ref[:, :, cols].reshape(128, 128)
            send[q][j * 128 : (j + 1) * 128, :] = block.T

    def copy_in(q, device, d):
        return pltpu.make_async_remote_copy(
            src_ref=send[q].at[pl.ds(pl.multiple_of(d * ROWS, ROWS), ROWS)],
            dst_ref=recv[q].at[pl.ds(pl.multiple_of(me * ROWS, ROWS), ROWS)],
            send_sem=in_send.at[q],
            recv_sem=in_recv.at[q],
            device_id=device,
            device_id_type=MESH,
        )

    def copy_out(q, device, d):
        return pltpu.make_async_remote_copy(
            src_ref=back[q].at[pl.ds(pl.multiple_of(d * ROWS, ROWS), ROWS)],
            dst_ref=final[q].at[pl.ds(pl.multiple_of(me * ROWS, ROWS), ROWS)],
            send_sem=out_send.at[q],
            recv_sem=out_recv.at[q],
            device_id=device,
            device_id_type=MESH,
        )

    def copy_target(device, d):
        return pltpu.make_async_remote_copy(
            src_ref=tsend.at[d // 16],
            dst_ref=trecv.at[me],
            send_sem=tsend_sem,
            recv_sem=trecv_sem,
            device_id=device,
            device_id_type=MESH,
        )

    def all_of(ref, sem):
        part = ref.at[pl.ds(0, PEERS * ROWS)]
        return pltpu.make_async_copy(part, part, sem)

    def all_targets(sem):
        part = trecv.at[pl.ds(0, PEERS)]
        return pltpu.make_async_copy(part, part, sem)

    turn_in(0)
    pl.semaphore_wait(barrier, PEERS)
    each_peer(lambda device, d: copy_target(device, d).start())
    each_peer(lambda device, d: copy_in(0, device, d).start())
    turn_in(1)
    each_peer(lambda device, d: copy_in(1, device, d).start())
    own = pl.ds(pl.multiple_of(me * ROWS, ROWS), ROWS)
    for q in range(CHUNKS):
        recv[q][own, :] = send[q][own, :]
    trecv[me] = tsend[me // 16]

    for k in range(9):
        level, s = divmod(k, 3)
        for c in range(2):
            re = interp_ref[level, s, c, 0]
            im = interp_ref[level, s, c, 1]
            wide[0:64, 0:64] = re
            wide[0:64, 64:128] = -im
            wide[64:128, 0:64] = im
            wide[64:128, 64:128] = re
            w = wide[...].T
            hi = w.astype(jnp.bfloat16)
            lo = (w - hi.astype(jnp.float32)).astype(jnp.bfloat16)
            rows = slice(c * 128, (c + 1) * 128)
            weights[k, rows, 0:128] = hi
            weights[k, rows, 128:256] = lo
    for level in range(3):
        for s in range(3):
            f = freq_ref[level, s].astype(jnp.float32) * (1.0 / 1024.0)
            k = (level * 3 + s) * 2
            freqs[k : k + 2, 0:64] = f
            freqs[k : k + 2, 64:128] = f

    lane = lax.broadcasted_iota(jnp.int32, (8, 128), 1)
    row = lax.broadcasted_iota(jnp.int32, (8, 128), 0)
    mine = lane == (me % 16) * ROWS + row
    all_targets(trecv_sem).wait()
    for q in range(CHUNKS):

        def gather(i, carry, q=q):
            t = trecv[i, q : q + 1, :]
            t = jnp.sum(jnp.where(mine, t, 0.0), axis=1, keepdims=True)
            turns[pl.ds(pl.multiple_of(q * half + i * 8, 8), 8), :] = jnp.broadcast_to(t, (8, 128))
            return carry

        lax.fori_loop(0, GROUP, gather, 0, unroll=8)

    lane1 = lax.broadcasted_iota(jnp.int32, (1, 128), 1)
    quarter = jnp.where(lane1 < 64, 0.0, -0.25)

    def fill(q, first, last):
        def body(i, carry):
            rows = pl.ds(pl.multiple_of(q * half + i * 64, 64), 64)
            t = turns[rows, :]
            low_half = lax.broadcasted_iota(jnp.int32, t.shape, 1) < 64
            for k in range(18):
                p = turn_cos(t * freqs[k : k + 1, :] + quarter)
                other = pltpu.roll(p, 64, 1)
                cosines[k, rows, :] = jnp.where(low_half, p, other)
                sines[k, rows, :] = jnp.where(low_half, -other, p)
            return carry

        lax.fori_loop(first, last, body, 0)

    def mix(k, rows, child0, child1):
        rot = []
        for c, x in enumerate((child0, child1)):
            rot.append(cosines[2 * k + c, rows, :] * x + sines[2 * k + c, rows, :] * pltpu.roll(x, 64, 1))
        rot = jnp.concatenate(rot, axis=1)
        hi = rot.astype(jnp.bfloat16)
        lo = (rot - hi.astype(jnp.float32)).astype(jnp.bfloat16)
        both = jnp.dot(hi, weights[k], preferred_element_type=jnp.float32)
        rest = jnp.dot(lo, weights[k, :, 0:128], preferred_element_type=jnp.float32)
        return both[:, 0:128] + both[:, 128:256] + rest

    def step(k, q, src, dst):
        stride = ROWS << STEP_BITS[k]
        base = q * half
        if stride >= BLOCK:
            for at in range(0, half, BLOCK):
                if at & stride == 0:
                    x0 = src[at : at + BLOCK, :]
                    x1 = src[at + stride : at + stride + BLOCK, :]
                    for here in (at, at + stride):
                        dst[here : here + BLOCK, :] = mix(
                            k, slice(base + here, base + here + BLOCK), x0, x1
                        )
        else:
            for at in range(0, half, BLOCK):
                x = src[at : at + BLOCK, :].reshape(BLOCK // (2 * stride), 2, stride, 128)
                children = [
                    jnp.broadcast_to(x[:, c : c + 1], x.shape).reshape(BLOCK, 128) for c in range(2)
                ]
                dst[at : at + BLOCK, :] = mix(k, slice(base + at, base + at + BLOCK), *children)

    fill(0, 0, half // 64)
    fill(1, 0, half // 128)
    for q in range(CHUNKS):
        all_of(recv[q], in_recv.at[q]).wait()
        states = [recv[q]] + [(state0, state1)[k % 2] for k in range(8)] + [back[q]]
        for k in range(9):
            step(k, q, states[k], states[k + 1])
        each_peer(lambda device, d, q=q: copy_out(q, device, d).start())
        final[q][own, :] = back[q][own, :]
        if q == 0:
            fill(1, half // 128, half // 64)

    def store(q):
        cols = pl.ds(q * half, half)
        return pltpu.make_async_copy(
            y_ref.at[:, :, cols], out_ref.at[:, :, cols], store_sem.at[q]
        )

    for q in range(CHUNKS):
        all_of(final[q], out_recv.at[q]).wait()
        for j in range(half // 128):
            block = final[q][j * 128 : (j + 1) * 128, :]
            cols = slice(q * half + j * 128, q * half + (j + 1) * 128)
            y_ref[:, :, cols] = block.T.reshape(2, 64, 128)
        store(q).start()
    all_targets(tsend_sem).wait()
    for q in range(CHUNKS):
        all_of(send[q], in_send.at[q]).wait()
        all_of(back[q], out_send.at[q]).wait()
        store(q).wait()


def shards(coeffs, interp, freq_index, target):
    f32 = jnp.float32
    anywhere = pl.BlockSpec(memory_space=pl.ANY)
    vmem = pl.BlockSpec(memory_space=pltpu.VMEM)
    big = pltpu.VMEM((CHUNK, 128), f32)
    dma = pltpu.SemaphoreType.DMA
    return pl.pallas_call(
        kernel,
        out_shape=jax.ShapeDtypeStruct(coeffs.shape, f32),
        in_specs=[anywhere, vmem, vmem, vmem],
        out_specs=anywhere,
        scratch_shapes=[
            pltpu.VMEM(coeffs.shape, f32),
            big, big, big, big, big, big, big, big, big, big,
            pltpu.VMEM(coeffs.shape, f32),
            pltpu.VMEM((8, CHUNKS, 128), f32),
            pltpu.VMEM((GROUP, CHUNKS, 128), f32),
            pltpu.VMEM((CHUNKS * CHUNK, 128), f32),
            pltpu.VMEM((24, 128), f32),
            pltpu.VMEM((128, 128), f32),
            pltpu.VMEM((9, 256, 256), jnp.bfloat16),
            pltpu.VMEM((18, CHUNKS * CHUNK, 128), f32),
            pltpu.VMEM((18, CHUNKS * CHUNK, 128), f32),
            dma((CHUNKS,)), dma((CHUNKS,)), dma, dma,
            dma((CHUNKS,)), dma((CHUNKS,)), dma((CHUNKS,)), dma((CHUNKS,)),
        ],
        compiler_params=pltpu.CompilerParams(
            collective_id=0, has_side_effects=True, vmem_limit_bytes=60 * 1024 * 1024
        ),
        name="butterfly",
    )(coeffs, interp, freq_index, target.reshape(16, 128))


def solution(mesh):
    in_specs = (P(None, None, ("gx", "gy", "gz")), P(), P(), P(("gx", "gy", "gz")))
    out_specs = P(None, None, ("gx", "gy", "gz"))
    return jax.shard_map(shards, mesh=mesh, in_specs=in_specs, out_specs=out_specs, check_vma=False)
```

```python
import functools
import math

import jax
import jax.numpy as jnp
import numpy as np
from jax import lax
from jax.experimental import pallas as pl
from jax.experimental.pallas import tpu as pltpu
from jax.sharding import PartitionSpec as P

MESH = pl.DeviceIdType.MESH
GROUP = 128
PEERS = GROUP - 1
CHUNKS = 2
ROWS = 8
CHUNK = GROUP * ROWS
STEP_BITS = (6, 2, 0, 5, 3, 1, 4, 2, 0)
BLOCK = 256
TURN = 512


def turn_cos_coefficients(degree=6):
    nodes = np.cos((np.arange(400) + 0.5) * np.pi / 400)
    z = (nodes + 1) / 8
    cheb = np.polynomial.chebyshev.Chebyshev.fit(
        z, np.cos(2 * np.pi * np.sqrt(z)), degree, domain=[0, 0.25]
    )
    poly = cheb.convert(kind=np.polynomial.Polynomial, domain=[-1, 1], window=[-1, 1])
    return [float(c) for c in poly.coef]


COS = turn_cos_coefficients()


def turn_cos(r):
    x = r - jnp.round(r)
    z = x * x
    acc = jnp.full_like(z, COS[-1])
    for c in COS[-2::-1]:
        acc = acc * z + c
    return acc


def place():
    gx, gy, gz = lax.axis_index("gx"), lax.axis_index("gy"), lax.axis_index("gz")
    return gx // 8, (gx // 2) % 4, gy, gz, gx % 2


def number(xlo, z, y, g):
    return ((xlo * 4 + z) * 4 + y) * 4 + g


def each_peer(fn):
    xlo, z, y, g, low = place()
    xs = [(xlo + i) % 2 for i in range(2)]
    zs = [(z + i) % 4 for i in range(4)]
    ys = [(y + i) % 4 for i in range(4)]
    gs = [(g + i) % 4 for i in range(4)]
    for dz in (2, 1, 3, 0):
        for dx in range(2):
            gx = xs[dx] * 8 + zs[dz] * 2 + low
            first = number(xs[dx], zs[dz], 0, 0)
            for dy in range(4):
                for dg in range(4):
                    if dz or dx or dy or dg:
                        fn((gx, ys[dy], gs[dg]), first + ys[dy] * 4 + gs[dg])


def kernel(
    coeffs_ref, interp_hbm, freq_hbm, target_hbm, rows_ref,
    x_ref, send0, send1, recv0, recv1, state0, state1, back0, back1,
    interp_ref, freq_ref, target_ref,
    tsend, trecv, turns, freqs, wide, weights, cosines, sines,
    load_sem, small_sem, own_sem, tsend_sem, trecv_sem, in_send, in_recv, out_send, out_recv,
):
    xlo, z, y, g, low = place()
    me = number(xlo, z, y, g)
    send, recv, back = (send0, send1), (recv0, recv1), (back0, back1)
    own = pl.ds(pl.multiple_of(me * ROWS, ROWS), ROWS)
    half = CHUNK

    def load(q):
        cols = pl.ds(q * half, half)
        return pltpu.make_async_copy(
            coeffs_ref.at[:, :, cols], x_ref.at[:, :, cols], load_sem.at[q]
        )

    barrier = pltpu.get_barrier_semaphore()
    each_peer(
        lambda device, d: pl.semaphore_signal(
            barrier, inc=1, device_id=device, device_id_type=MESH
        )
    )

    small = [
        pltpu.make_async_copy(src, dst, small_sem.at[i])
        for i, (src, dst) in enumerate(
            ((target_hbm, target_ref), (freq_hbm, freq_ref), (interp_hbm, interp_ref))
        )
    ]
    small[0].start()
    for q in range(CHUNKS):
        load(q).start()
    small[1].start()
    small[2].start()

    small[0].wait()
    targets = target_ref[...].astype(jnp.float32)
    for k in range(8):
        for q in range(CHUNKS):
            tsend[k, q : q + 1, :] = targets[q * 8 + k : q * 8 + k + 1, :]

    def turn_in(q):
        load(q).wait()
        for j in range(half // 128):
            cols = slice(q * half + j * 128, q * half + (j + 1) * 128)
            block = x_ref[:, :, cols].reshape(128, 128)
            send[q][j * 128 : (j + 1) * 128, :] = block.T

    def copy_in(q, device, d):
        return pltpu.make_async_remote_copy(
            src_ref=send[q].at[pl.ds(pl.multiple_of(d * ROWS, ROWS), ROWS)],
            dst_ref=recv[q].at[pl.ds(pl.multiple_of(me * ROWS, ROWS), ROWS)],
            send_sem=in_send.at[q],
            recv_sem=in_recv.at[q],
            device_id=device,
            device_id_type=MESH,
        )

    def copy_out(q, device, d):
        return pltpu.make_async_remote_copy(
            src_ref=back[q].at[pl.ds(pl.multiple_of(d * ROWS, ROWS), ROWS)],
            dst_ref=rows_ref.at[pl.ds(pl.multiple_of(q * CHUNK + me * ROWS, ROWS), ROWS)],
            send_sem=out_send.at[q],
            recv_sem=out_recv.at[q],
            device_id=device,
            device_id_type=MESH,
        )

    def copy_target(device, d):
        return pltpu.make_async_remote_copy(
            src_ref=tsend.at[d // 16],
            dst_ref=trecv.at[me],
            send_sem=tsend_sem,
            recv_sem=trecv_sem,
            device_id=device,
            device_id_type=MESH,
        )

    def keep(q):
        return pltpu.make_async_copy(
            back[q].at[own],
            rows_ref.at[pl.ds(pl.multiple_of(q * CHUNK + me * ROWS, ROWS), ROWS)],
            own_sem.at[q],
        )

    def all_of(ref, sem):
        part = ref.at[pl.ds(0, PEERS * ROWS)]
        return pltpu.make_async_copy(part, part, sem)

    def all_targets(sem):
        part = trecv.at[pl.ds(0, PEERS)]
        return pltpu.make_async_copy(part, part, sem)

    turn_in(0)
    pl.semaphore_wait(barrier, PEERS)
    each_peer(lambda device, d: copy_target(device, d).start())
    each_peer(lambda device, d: copy_in(0, device, d).start())
    turn_in(1)
    each_peer(lambda device, d: copy_in(1, device, d).start())
    for q in range(CHUNKS):
        recv[q][own, :] = send[q][own, :]
    trecv[me] = tsend[me // 16]

    small[1].wait()
    small[2].wait()
    for k in range(9):
        level, s = divmod(k, 3)
        for c in range(2):
            re = interp_ref[level, s, c, 0]
            im = interp_ref[level, s, c, 1]
            wide[0:64, 0:64] = re
            wide[0:64, 64:128] = -im
            wide[64:128, 0:64] = im
            wide[64:128, 64:128] = re
            w = wide[...].T
            hi = w.astype(jnp.bfloat16)
            lo = (w - hi.astype(jnp.float32)).astype(jnp.bfloat16)
            rows = slice(c * 128, (c + 1) * 128)
            weights[k, rows, 0:128] = hi
            weights[k, rows, 128:256] = lo
    for level in range(3):
        for s in range(3):
            f = freq_ref[level, s].astype(jnp.float32) * (1.0 / 1024.0)
            k = (level * 3 + s) * 2
            freqs[k : k + 2, 0:64] = f
            freqs[k : k + 2, 64:128] = f

    lane = lax.broadcasted_iota(jnp.int32, (8, 128), 1)
    row = lax.broadcasted_iota(jnp.int32, (8, 128), 0)
    mine = lane == (me % 16) * ROWS + row
    all_targets(trecv_sem).wait()
    for q in range(CHUNKS):

        def gather(i, carry, q=q):
            t = trecv[i, q : q + 1, :]
            t = jnp.sum(jnp.where(mine, t, 0.0), axis=1, keepdims=True)
            turns[pl.ds(pl.multiple_of(q * half + i * 8, 8), 8), :] = jnp.broadcast_to(t, (8, 128))
            return carry

        lax.fori_loop(0, GROUP, gather, 0, unroll=8)

    lane1 = lax.broadcasted_iota(jnp.int32, (1, 128), 1)
    quarter = jnp.where(lane1 < 64, 0.0, -0.25)

    def fill(q, first, last):
        def body(i, carry):
            rows = pl.ds(pl.multiple_of(q * half + i * 64, 64), 64)
            t = turns[rows, :]
            low_half = lax.broadcasted_iota(jnp.int32, t.shape, 1) < 64
            for k in range(18):
                p = turn_cos(t * freqs[k : k + 1, :] + quarter)
                other = pltpu.roll(p, 64, 1)
                cosines[k, rows, :] = jnp.where(low_half, p, other)
                sines[k, rows, :] = jnp.where(low_half, -other, p)
            return carry

        lax.fori_loop(first, last, body, 0)

    def mix(k, rows, child0, child1):
        rot = []
        for c, x in enumerate((child0, child1)):
            rot.append(cosines[2 * k + c, rows, :] * x + sines[2 * k + c, rows, :] * pltpu.roll(x, 64, 1))
        rot = jnp.concatenate(rot, axis=1)
        hi = rot.astype(jnp.bfloat16)
        lo = (rot - hi.astype(jnp.float32)).astype(jnp.bfloat16)
        both = jnp.dot(hi, weights[k], preferred_element_type=jnp.float32)
        rest = jnp.dot(lo, weights[k, :, 0:128], preferred_element_type=jnp.float32)
        return both[:, 0:128] + both[:, 128:256] + rest

    def step(k, q, src, dst):
        stride = ROWS << STEP_BITS[k]
        base = q * half
        if stride >= BLOCK:
            for at in range(0, half, BLOCK):
                if at & stride == 0:
                    x0 = src[at : at + BLOCK, :]
                    x1 = src[at + stride : at + stride + BLOCK, :]
                    for here in (at, at + stride):
                        dst[here : here + BLOCK, :] = mix(
                            k, slice(base + here, base + here + BLOCK), x0, x1
                        )
        else:
            for at in range(0, half, BLOCK):
                x = src[at : at + BLOCK, :].reshape(BLOCK // (2 * stride), 2, stride, 128)
                children = [
                    jnp.broadcast_to(x[:, c : c + 1], x.shape).reshape(BLOCK, 128) for c in range(2)
                ]
                dst[at : at + BLOCK, :] = mix(k, slice(base + at, base + at + BLOCK), *children)

    fill(0, 0, half // 64)
    for q in range(CHUNKS):
        all_of(recv[q], in_recv.at[q]).wait()
        states = [recv[q]] + [(state0, state1)[k % 2] for k in range(8)] + [back[q]]
        for k in range(9):
            step(k, q, states[k], states[k + 1])
        each_peer(lambda device, d, q=q: copy_out(q, device, d).start())
        keep(q).start()
        if q == 0:
            fill(1, 0, half // 64)

    for q in range(CHUNKS):
        all_of(rows_ref, out_recv.at[q]).wait()
        keep(q).wait()
    all_targets(tsend_sem).wait()
    for q in range(CHUNKS):
        all_of(send[q], in_send.at[q]).wait()
        all_of(back[q], out_send.at[q]).wait()


def turn_kernel(rows_ref, out_ref):
    for j in range(TURN // 128):
        block = rows_ref[pl.ds(pl.multiple_of(pl.program_id(0) * TURN + j * 128, 128), 128), :]
        out_ref[:, :, j * 128 : (j + 1) * 128] = block.T.reshape(2, 64, 128)


def shards(coeffs, interp, freq_index, target):
    f32 = jnp.float32
    anywhere = pl.BlockSpec(memory_space=pl.ANY)
    big = pltpu.VMEM((CHUNK, 128), f32)
    dma = pltpu.SemaphoreType.DMA
    positions = coeffs.shape[2]
    rows = pl.pallas_call(
        kernel,
        out_shape=jax.ShapeDtypeStruct((positions, 128), f32),
        in_specs=[pl.BlockSpec(memory_space=pltpu.HBM)] * 4,
        out_specs=anywhere,
        scratch_shapes=[
            pltpu.VMEM(coeffs.shape, f32),
            big, big, big, big, big, big, big, big,
            pltpu.VMEM(interp.shape, f32),
            pltpu.VMEM(freq_index.shape, jnp.int32),
            pltpu.VMEM((16, 128), jnp.int32),
            pltpu.VMEM((8, CHUNKS, 128), f32),
            pltpu.VMEM((GROUP, CHUNKS, 128), f32),
            pltpu.VMEM((CHUNKS * CHUNK, 128), f32),
            pltpu.VMEM((24, 128), f32),
            pltpu.VMEM((128, 128), f32),
            pltpu.VMEM((9, 256, 256), jnp.bfloat16),
            pltpu.VMEM((18, CHUNKS * CHUNK, 128), f32),
            pltpu.VMEM((18, CHUNKS * CHUNK, 128), f32),
            dma((CHUNKS,)), dma((3,)), dma((CHUNKS,)), dma, dma,
            dma((CHUNKS,)), dma((CHUNKS,)), dma((CHUNKS,)), dma((CHUNKS,)),
        ],
        compiler_params=pltpu.CompilerParams(
            collective_id=0, has_side_effects=True, vmem_limit_bytes=52 * 1024 * 1024
        ),
        name="butterfly",
    )(*(
        pltpu.with_memory_space_constraint(x, pltpu.HBM)
        for x in (coeffs, interp, freq_index, target.reshape(16, 128))
    ))
    rows = pltpu.with_memory_space_constraint(rows, pltpu.VMEM)
    return pl.pallas_call(
        turn_kernel,
        grid=(positions // TURN,),
        out_shape=jax.ShapeDtypeStruct(coeffs.shape, f32),
        in_specs=[pl.BlockSpec(memory_space=pltpu.VMEM)],
        out_specs=pl.BlockSpec((2, 64, TURN), lambda i: (0, 0, i)),
        name="turn",
    )(rows)


def solution(mesh):
    in_specs = (P(None, None, ("gx", "gy", "gz")), P(), P(), P(("gx", "gy", "gz")))
    out_specs = P(None, None, ("gx", "gy", "gz"))
    return jax.shard_map(shards, mesh=mesh, in_specs=in_specs, out_specs=out_specs, check_vma=False)
```

```python
import functools
import math

import jax
import jax.numpy as jnp
import numpy as np
from jax import lax
from jax.experimental import pallas as pl
from jax.experimental.pallas import tpu as pltpu
from jax.sharding import PartitionSpec as P

MESH = pl.DeviceIdType.MESH
GROUP = 128
PEERS = GROUP - 1
CHUNKS = 2
ROWS = 8
CHUNK = GROUP * ROWS
STEP_BITS = (6, 2, 0, 5, 3, 1, 4, 2, 0)
BLOCK = 256
TURN = 512


def turn_cos_coefficients(degree=6):
    nodes = np.cos((np.arange(400) + 0.5) * np.pi / 400)
    z = (nodes + 1) / 8
    cheb = np.polynomial.chebyshev.Chebyshev.fit(
        z, np.cos(2 * np.pi * np.sqrt(z)), degree, domain=[0, 0.25]
    )
    poly = cheb.convert(kind=np.polynomial.Polynomial, domain=[-1, 1], window=[-1, 1])
    return [float(c) for c in poly.coef]


COS = turn_cos_coefficients()


def turn_cos(r):
    x = r - jnp.round(r)
    z = x * x
    acc = jnp.full_like(z, COS[-1])
    for c in COS[-2::-1]:
        acc = acc * z + c
    return acc


def place():
    gx, gy, gz = lax.axis_index("gx"), lax.axis_index("gy"), lax.axis_index("gz")
    return gx // 8, (gx // 2) % 4, gy, gz, gx % 2


def number(xlo, z, y, g):
    return ((xlo * 4 + z) * 4 + y) * 4 + g


def each_peer(fn):
    xlo, z, y, g, low = place()
    xs = [(xlo + i) % 2 for i in range(2)]
    zs = [(z + i) % 4 for i in range(4)]
    ys = [(y + i) % 4 for i in range(4)]
    gs = [(g + i) % 4 for i in range(4)]
    for dzs in ((2,), (1, 3), (0,)):
        for dx in range(2):
            for dy in range(4):
                for dg in range(4):
                    for dz in dzs:
                        if dz or dx or dy or dg:
                            gx = xs[dx] * 8 + zs[dz] * 2 + low
                            first = number(xs[dx], zs[dz], 0, 0)
                            fn((gx, ys[dy], gs[dg]), first + ys[dy] * 4 + gs[dg])


def kernel(
    coeffs_ref, interp_hbm, freq_hbm, target_hbm, rows_ref,
    x_ref, send, recv0, recv1, state0, state1, back0, back1,
    interp_ref, freq_ref, target_ref,
    tsend, trecv, turns, freqs, wide, weights, cosines, sines,
    load_sem, small_sem, own_sem, tsend_sem, trecv_sem, in_send, in_recv, out_send, out_recv,
):
    xlo, z, y, g, low = place()
    me = number(xlo, z, y, g)
    recv, back = (recv0, recv1), (back0, back1)
    own = pl.ds(pl.multiple_of(me * ROWS, ROWS), ROWS)
    half = CHUNK

    def home(q, d):
        return pl.ds(pl.multiple_of((d * CHUNKS + q) * ROWS, ROWS), ROWS)

    def load(q):
        cols = pl.ds(q * half, half)
        return pltpu.make_async_copy(
            coeffs_ref.at[:, :, cols], x_ref.at[:, :, cols], load_sem.at[q]
        )

    barrier = pltpu.get_barrier_semaphore()
    each_peer(
        lambda device, d: pl.semaphore_signal(
            barrier, inc=1, device_id=device, device_id_type=MESH
        )
    )

    small = [
        pltpu.make_async_copy(src, dst, small_sem.at[i])
        for i, (src, dst) in enumerate(
            ((target_hbm, target_ref), (freq_hbm, freq_ref), (interp_hbm, interp_ref))
        )
    ]
    small[0].start()
    for q in range(CHUNKS):
        load(q).start()
    small[1].start()
    small[2].start()

    small[0].wait()
    targets = target_ref[...].astype(jnp.float32)
    for k in range(16):
        tsend[k] = targets[k : k + 1, :]

    def turn_in(q):
        load(q).wait()
        for j in range(half // 128):
            cols = slice(q * half + j * 128, q * half + (j + 1) * 128)
            block = x_ref[:, :, cols].reshape(128, 128)
            send[q * half + j * 128 : q * half + (j + 1) * 128, :] = block.T

    def copy_in(q, device, d):
        return pltpu.make_async_remote_copy(
            src_ref=send.at[home(q, d)],
            dst_ref=recv[q].at[pl.ds(pl.multiple_of(me * ROWS, ROWS), ROWS)],
            send_sem=in_send.at[q],
            recv_sem=in_recv.at[q],
            device_id=device,
            device_id_type=MESH,
        )

    def copy_out(q, device, d):
        return pltpu.make_async_remote_copy(
            src_ref=back[q].at[pl.ds(pl.multiple_of(d * ROWS, ROWS), ROWS)],
            dst_ref=rows_ref.at[home(q, me)],
            send_sem=out_send.at[q],
            recv_sem=out_recv.at[q],
            device_id=device,
            device_id_type=MESH,
        )

    def copy_target(device, d):
        return pltpu.make_async_remote_copy(
            src_ref=tsend.at[d // 8],
            dst_ref=trecv.at[me],
            send_sem=tsend_sem,
            recv_sem=trecv_sem,
            device_id=device,
            device_id_type=MESH,
        )

    def keep(q):
        return pltpu.make_async_copy(
            back[q].at[own],
            rows_ref.at[home(q, me)],
            own_sem.at[q],
        )

    def all_of(ref, sem):
        part = ref.at[pl.ds(0, PEERS * ROWS)]
        return pltpu.make_async_copy(part, part, sem)

    def all_targets(sem):
        part = trecv.at[pl.ds(0, PEERS)]
        return pltpu.make_async_copy(part, part, sem)

    turn_in(0)
    turn_in(1)
    pl.semaphore_wait(barrier, PEERS)
    each_peer(lambda device, d: copy_target(device, d).start())
    each_peer(lambda device, d: copy_in(0, device, d).start())
    each_peer(lambda device, d: copy_in(1, device, d).start())
    for q in range(CHUNKS):
        recv[q][own, :] = send[home(q, me), :]
    trecv[me] = tsend[me // 8]

    small[1].wait()
    small[2].wait()
    for k in range(9):
        level, s = divmod(k, 3)
        for c in range(2):
            re = interp_ref[level, s, c, 0]
            im = interp_ref[level, s, c, 1]
            wide[0:64, 0:64] = re
            wide[0:64, 64:128] = -im
            wide[64:128, 0:64] = im
            wide[64:128, 64:128] = re
            w = wide[...].T
            hi = w.astype(jnp.bfloat16)
            lo = (w - hi.astype(jnp.float32)).astype(jnp.bfloat16)
            rows = slice(c * 128, (c + 1) * 128)
            weights[k, rows, 0:128] = hi
            weights[k, rows, 128:256] = lo
    for level in range(3):
        for s in range(3):
            f = freq_ref[level, s].astype(jnp.float32) * (1.0 / 1024.0)
            k = (level * 3 + s) * 2
            freqs[k : k + 2, 0:64] = f
            freqs[k : k + 2, 64:128] = f

    lane = lax.broadcasted_iota(jnp.int32, (8, 128), 1)
    row = lax.broadcasted_iota(jnp.int32, (8, 128), 0)
    all_targets(trecv_sem).wait()
    for q in range(CHUNKS):

        mine = lane == (me % 8) * (CHUNKS * ROWS) + q * ROWS + row

        def gather(i, carry, q=q, mine=mine):
            t = trecv[i]
            t = jnp.sum(jnp.where(mine, t, 0.0), axis=1, keepdims=True)
            turns[pl.ds(pl.multiple_of(q * half + i * 8, 8), 8), :] = jnp.broadcast_to(t, (8, 128))
            return carry

        lax.fori_loop(0, GROUP, gather, 0, unroll=8)

    lane1 = lax.broadcasted_iota(jnp.int32, (1, 128), 1)
    quarter = jnp.where(lane1 < 64, 0.0, -0.25)

    def fill(q, first, last):
        def body(i, carry):
            rows = pl.ds(pl.multiple_of(q * half + i * 64, 64), 64)
            t = turns[rows, :]
            low_half = lax.broadcasted_iota(jnp.int32, t.shape, 1) < 64
            for k in range(18):
                p = turn_cos(t * freqs[k : k + 1, :] + quarter)
                other = pltpu.roll(p, 64, 1)
                cosines[k, rows, :] = jnp.where(low_half, p, other)
                sines[k, rows, :] = jnp.where(low_half, -other, p)
            return carry

        lax.fori_loop(first, last, body, 0)

    def mix(k, rows, child0, child1):
        rot = []
        for c, x in enumerate((child0, child1)):
            rot.append(cosines[2 * k + c, rows, :] * x + sines[2 * k + c, rows, :] * pltpu.roll(x, 64, 1))
        rot = jnp.concatenate(rot, axis=1)
        hi = rot.astype(jnp.bfloat16)
        lo = (rot - hi.astype(jnp.float32)).astype(jnp.bfloat16)
        both = jnp.dot(hi, weights[k], preferred_element_type=jnp.float32)
        rest = jnp.dot(lo, weights[k, :, 0:128], preferred_element_type=jnp.float32)
        return both[:, 0:128] + both[:, 128:256] + rest

    def step(k, q, src, dst):
        stride = ROWS << STEP_BITS[k]
        base = q * half
        if stride >= BLOCK:
            for at in range(0, half, BLOCK):
                if at & stride == 0:
                    x0 = src[at : at + BLOCK, :]
                    x1 = src[at + stride : at + stride + BLOCK, :]
                    for here in (at, at + stride):
                        dst[here : here + BLOCK, :] = mix(
                            k, slice(base + here, base + here + BLOCK), x0, x1
                        )
        else:
            for at in range(0, half, BLOCK):
                x = src[at : at + BLOCK, :].reshape(BLOCK // (2 * stride), 2, stride, 128)
                children = [
                    jnp.broadcast_to(x[:, c : c + 1], x.shape).reshape(BLOCK, 128) for c in range(2)
                ]
                dst[at : at + BLOCK, :] = mix(k, slice(base + at, base + at + BLOCK), *children)

    fill(0, 0, half // 64)
    for q in range(CHUNKS):
        all_of(recv[q], in_recv.at[q]).wait()
        states = [recv[q]] + [(state0, state1)[k % 2] for k in range(8)] + [back[q]]
        for k in range(9):
            step(k, q, states[k], states[k + 1])
        each_peer(lambda device, d, q=q: copy_out(q, device, d).start())
        keep(q).start()
        if q == 0:
            fill(1, 0, half // 64)

    for q in range(CHUNKS):
        all_of(rows_ref, out_recv.at[q]).wait()
        keep(q).wait()
    all_targets(tsend_sem).wait()
    for q in range(CHUNKS):
        all_of(send, in_send.at[q]).wait()
        all_of(back[q], out_send.at[q]).wait()


def turn_kernel(rows_ref, out_ref):
    for j in range(TURN // 128):
        block = rows_ref[pl.ds(pl.multiple_of(pl.program_id(0) * TURN + j * 128, 128), 128), :]
        out_ref[:, :, j * 128 : (j + 1) * 128] = block.T.reshape(2, 64, 128)


def shards(coeffs, interp, freq_index, target):
    f32 = jnp.float32
    anywhere = pl.BlockSpec(memory_space=pl.ANY)
    big = pltpu.VMEM((CHUNK, 128), f32)
    dma = pltpu.SemaphoreType.DMA
    positions = coeffs.shape[2]
    rows = pl.pallas_call(
        kernel,
        out_shape=jax.ShapeDtypeStruct((positions, 128), f32),
        in_specs=[pl.BlockSpec(memory_space=pltpu.HBM)] * 4,
        out_specs=anywhere,
        scratch_shapes=[
            pltpu.VMEM(coeffs.shape, f32),
            pltpu.VMEM((CHUNKS * CHUNK, 128), f32),
            big, big, big, big, big, big,
            pltpu.VMEM(interp.shape, f32),
            pltpu.VMEM(freq_index.shape, jnp.int32),
            pltpu.VMEM((16, 128), jnp.int32),
            pltpu.VMEM((16, 1, 128), f32),
            pltpu.VMEM((GROUP, 1, 128), f32),
            pltpu.VMEM((CHUNKS * CHUNK, 128), f32),
            pltpu.VMEM((24, 128), f32),
            pltpu.VMEM((128, 128), f32),
            pltpu.VMEM((9, 256, 256), jnp.bfloat16),
            pltpu.VMEM((18, CHUNKS * CHUNK, 128), f32),
            pltpu.VMEM((18, CHUNKS * CHUNK, 128), f32),
            dma((CHUNKS,)), dma((3,)), dma((CHUNKS,)), dma, dma,
            dma((CHUNKS,)), dma((CHUNKS,)), dma((CHUNKS,)), dma((CHUNKS,)),
        ],
        compiler_params=pltpu.CompilerParams(
            collective_id=0, has_side_effects=True, vmem_limit_bytes=52 * 1024 * 1024
        ),
        name="butterfly",
    )(*(
        pltpu.with_memory_space_constraint(x, pltpu.HBM)
        for x in (coeffs, interp, freq_index, target.reshape(16, 128))
    ))
    rows = pltpu.with_memory_space_constraint(rows, pltpu.VMEM)
    return pl.pallas_call(
        turn_kernel,
        grid=(positions // TURN,),
        out_shape=jax.ShapeDtypeStruct(coeffs.shape, f32),
        in_specs=[pl.BlockSpec(memory_space=pltpu.VMEM)],
        out_specs=pl.BlockSpec((2, 64, TURN), lambda i: (0, 0, i)),
        name="turn",
    )(rows)


def solution(mesh):
    in_specs = (P(None, None, ("gx", "gy", "gz")), P(), P(), P(("gx", "gy", "gz")))
    out_specs = P(None, None, ("gx", "gy", "gz"))
    return jax.shard_map(shards, mesh=mesh, in_specs=in_specs, out_specs=out_specs, check_vma=False)
```

```python
import functools
import math

import jax
import jax.numpy as jnp
import numpy as np
from jax import lax
from jax.experimental import pallas as pl
from jax.experimental.pallas import tpu as pltpu
from jax.sharding import PartitionSpec as P

MESH = pl.DeviceIdType.MESH
GROUP = 128
PEERS = GROUP - 1
CHUNKS = 2
ROWS = 8
CHUNK = GROUP * ROWS
STEP_BITS = (6, 2, 0, 5, 3, 1, 4, 2, 0)
BLOCK = 256
TURN = 512


def turn_cos_coefficients(degree=6):
    nodes = np.cos((np.arange(400) + 0.5) * np.pi / 400)
    z = (nodes + 1) / 8
    cheb = np.polynomial.chebyshev.Chebyshev.fit(
        z, np.cos(2 * np.pi * np.sqrt(z)), degree, domain=[0, 0.25]
    )
    poly = cheb.convert(kind=np.polynomial.Polynomial, domain=[-1, 1], window=[-1, 1])
    return [float(c) for c in poly.coef]


COS = turn_cos_coefficients()


def turn_cos(r):
    x = r - jnp.round(r)
    z = x * x
    acc = jnp.full_like(z, COS[-1])
    for c in COS[-2::-1]:
        acc = acc * z + c
    return acc


def place():
    gx, gy, gz = lax.axis_index("gx"), lax.axis_index("gy"), lax.axis_index("gz")
    return gx // 8, (gx // 2) % 4, gy, gz, gx % 2


def number(xlo, z, y, g):
    return ((xlo * 4 + z) * 4 + y) * 4 + g


def plane(m):
    z = place()[1]
    return (z, z + 1 - 2 * (z % 2), (z + 2) % 4, 3 - z)[m]


def peers(*masks):
    xlo, z, y, g, low = place()
    xs = [(xlo + i) % 2 for i in range(2)]
    ys = [(y + i) % 4 for i in range(4)]
    gs = [(g + i) % 4 for i in range(4)]
    zs = {m: plane(m) for m in masks}
    out = []
    for i in range(32):
        dx, dy, dg = i // 16, i // 4 % 4, i % 4
        for m in masks:
            if m or i:
                device = (xs[dx] * 8 + zs[m] * 2 + low, ys[dy], gs[dg])
                out.append((device, number(xs[dx], zs[m], 0, 0) + ys[dy] * 4 + gs[dg]))
    return out


def all_peers():
    return peers(2) + peers(1, 3) + peers(0)


def kernel(
    coeffs_ref, interp_hbm, freq_hbm, target_hbm, rows_ref,
    x_ref, send, recv0, recv1, state0, state1, back0, back1,
    interp_ref, freq_ref, target_ref,
    tsend, trecv, turns, freqs, wide, weights, cosines, sines,
    ready, load_sem, small_sem, own_sem, tsend_sem, trecv_sem, in_send, in_recv, out_send, out_recv,
):
    xlo, z, y, g, low = place()
    me = number(xlo, z, y, g)
    recv, back = (recv0, recv1), (back0, back1)
    own = pl.ds(pl.multiple_of(me * ROWS, ROWS), ROWS)
    half = CHUNK

    def home(q, d):
        return pl.ds(pl.multiple_of((d * CHUNKS + q) * ROWS, ROWS), ROWS)

    def load(q):
        cols = pl.ds(q * half, half)
        return pltpu.make_async_copy(
            coeffs_ref.at[:, :, cols], x_ref.at[:, :, cols], load_sem.at[q]
        )

    barrier = pltpu.get_barrier_semaphore()
    above = [((xlo * 8 + plane(m) * 2 + low, y, g), m) for m in (1, 3, 2)]
    near = [device for device, _ in peers(0)] + [device for device, _ in above]
    for device in near:
        pl.semaphore_signal(barrier, inc=1, device_id=device, device_id_type=MESH)

    small = [
        pltpu.make_async_copy(src, dst, small_sem.at[i])
        for i, (src, dst) in enumerate(
            ((target_hbm, target_ref), (freq_hbm, freq_ref), (interp_hbm, interp_ref))
        )
    ]
    small[0].start()
    for q in range(CHUNKS):
        load(q).start()
    small[1].start()
    small[2].start()

    small[0].wait()
    targets = target_ref[...].astype(jnp.float32)
    for k in range(16):
        tsend[k] = targets[k : k + 1, :]

    def turn_in(q):
        load(q).wait()
        for j in range(half // 128):
            cols = slice(q * half + j * 128, q * half + (j + 1) * 128)
            block = x_ref[:, :, cols].reshape(128, 128)
            send[q * half + j * 128 : q * half + (j + 1) * 128, :] = block.T

    def copy_in(q, device, d):
        return pltpu.make_async_remote_copy(
            src_ref=send.at[home(q, d)],
            dst_ref=recv[q].at[pl.ds(pl.multiple_of(me * ROWS, ROWS), ROWS)],
            send_sem=in_send.at[q],
            recv_sem=in_recv.at[q],
            device_id=device,
            device_id_type=MESH,
        )

    def copy_out(q, device, d):
        return pltpu.make_async_remote_copy(
            src_ref=back[q].at[pl.ds(pl.multiple_of(d * ROWS, ROWS), ROWS)],
            dst_ref=rows_ref.at[home(q, me)],
            send_sem=out_send.at[q],
            recv_sem=out_recv.at[q],
            device_id=device,
            device_id_type=MESH,
        )

    def copy_target(m, device, d):
        return pltpu.make_async_remote_copy(
            src_ref=tsend.at[d // 8],
            dst_ref=trecv.at[me],
            send_sem=tsend_sem,
            recv_sem=trecv_sem.at[m],
            device_id=device,
            device_id_type=MESH,
        )

    def keep(q):
        return pltpu.make_async_copy(
            back[q].at[own],
            rows_ref.at[home(q, me)],
            own_sem.at[q],
        )

    def all_of(ref, sem):
        part = ref.at[pl.ds(0, PEERS * ROWS)]
        return pltpu.make_async_copy(part, part, sem)

    def all_targets(count, sem):
        part = trecv.at[pl.ds(0, count)]
        return pltpu.make_async_copy(part, part, sem)

    turn_in(0)
    turn_in(1)
    pl.semaphore_wait(barrier, len(near))
    for device, m in above:
        pl.semaphore_signal(ready.at[m], inc=1, device_id=device, device_id_type=MESH)
    for m in (0, 1, 3, 2):
        if m:
            pl.semaphore_wait(ready.at[m], 1)
        for device, d in peers(m):
            copy_target(m, device, d).start()
        for device, d in peers(m):
            copy_in(0, device, d).start()
    for device, d in all_peers():
        copy_in(1, device, d).start()
    for q in range(CHUNKS):
        recv[q][own, :] = send[home(q, me), :]
    trecv[me] = tsend[me // 8]

    small[1].wait()
    small[2].wait()
    for k in range(9):
        level, s = divmod(k, 3)
        for c in range(2):
            re = interp_ref[level, s, c, 0]
            im = interp_ref[level, s, c, 1]
            wide[0:64, 0:64] = re
            wide[0:64, 64:128] = -im
            wide[64:128, 0:64] = im
            wide[64:128, 64:128] = re
            w = wide[...].T
            hi = w.astype(jnp.bfloat16)
            lo = (w - hi.astype(jnp.float32)).astype(jnp.bfloat16)
            rows = slice(c * 128, (c + 1) * 128)
            weights[k, rows, 0:128] = hi
            weights[k, rows, 128:256] = lo
    for level in range(3):
        for s in range(3):
            f = freq_ref[level, s].astype(jnp.float32) * (1.0 / 1024.0)
            k = (level * 3 + s) * 2
            freqs[k : k + 2, 0:64] = f
            freqs[k : k + 2, 64:128] = f

    lane = lax.broadcasted_iota(jnp.int32, (8, 128), 1)
    row = lax.broadcasted_iota(jnp.int32, (8, 128), 0)

    def gather(q, first, count):
        mine = lane == (me % 8) * (CHUNKS * ROWS) + q * ROWS + row

        def body(i, carry):
            t = jnp.sum(jnp.where(mine, trecv[first + i], 0.0), axis=1, keepdims=True)
            rows = pl.ds(pl.multiple_of(q * half + (first + i) * 8, 8), 8)
            turns[rows, :] = jnp.broadcast_to(t, (8, 128))
            return carry

        lax.fori_loop(0, count, body, 0, unroll=8)

    lane1 = lax.broadcasted_iota(jnp.int32, (1, 128), 1)
    quarter = jnp.where(lane1 < 64, 0.0, -0.25)

    def fill(q, first, count):
        def body(i, carry):
            rows = pl.ds(pl.multiple_of(q * half + first * 8 + i * 64, 64), 64)
            t = turns[rows, :]
            low_half = lax.broadcasted_iota(jnp.int32, t.shape, 1) < 64
            for k in range(18):
                p = turn_cos(t * freqs[k : k + 1, :] + quarter)
                other = pltpu.roll(p, 64, 1)
                cosines[k, rows, :] = jnp.where(low_half, p, other)
                sines[k, rows, :] = jnp.where(low_half, -other, p)
            return carry

        lax.fori_loop(0, count // 8, body, 0)

    def mix(k, rows, child0, child1):
        rot = []
        for c, x in enumerate((child0, child1)):
            rot.append(cosines[2 * k + c, rows, :] * x + sines[2 * k + c, rows, :] * pltpu.roll(x, 64, 1))
        rot = jnp.concatenate(rot, axis=1)
        hi = rot.astype(jnp.bfloat16)
        lo = (rot - hi.astype(jnp.float32)).astype(jnp.bfloat16)
        both = jnp.dot(hi, weights[k], preferred_element_type=jnp.float32)
        rest = jnp.dot(lo, weights[k, :, 0:128], preferred_element_type=jnp.float32)
        return both[:, 0:128] + both[:, 128:256] + rest

    def step(k, q, src, dst):
        stride = ROWS << STEP_BITS[k]
        base = q * half
        if stride >= BLOCK:
            for at in range(0, half, BLOCK):
                if at & stride == 0:
                    x0 = src[at : at + BLOCK, :]
                    x1 = src[at + stride : at + stride + BLOCK, :]
                    for here in (at, at + stride):
                        dst[here : here + BLOCK, :] = mix(
                            k, slice(base + here, base + here + BLOCK), x0, x1
                        )
        else:
            for at in range(0, half, BLOCK):
                x = src[at : at + BLOCK, :].reshape(BLOCK // (2 * stride), 2, stride, 128)
                children = [
                    jnp.broadcast_to(x[:, c : c + 1], x.shape).reshape(BLOCK, 128) for c in range(2)
                ]
                dst[at : at + BLOCK, :] = mix(k, slice(base + at, base + at + BLOCK), *children)

    for m in (0, 1, 3, 2):
        all_targets(32 if m else 31, trecv_sem.at[m]).wait()

        def of_plane(x, carry, m=m):
            first = x * 64 + plane(m) * 16
            gather(0, first, 16)
            fill(0, first, 16)
            return carry

        lax.fori_loop(0, 2, of_plane, 0)
    for q in range(CHUNKS):
        all_of(recv[q], in_recv.at[q]).wait()
        states = [recv[q]] + [(state0, state1)[k % 2] for k in range(8)] + [back[q]]
        for k in range(9):
            step(k, q, states[k], states[k + 1])
        for device, d in all_peers():
            copy_out(q, device, d).start()
        keep(q).start()
        if q == 0:
            gather(1, 0, GROUP)
            fill(1, 0, GROUP)

    for q in range(CHUNKS):
        all_of(rows_ref, out_recv.at[q]).wait()
        keep(q).wait()
    all_targets(PEERS, tsend_sem).wait()
    for q in range(CHUNKS):
        all_of(send, in_send.at[q]).wait()
        all_of(back[q], out_send.at[q]).wait()


def turn_kernel(rows_ref, out_ref):
    for j in range(TURN // 128):
        block = rows_ref[pl.ds(pl.multiple_of(pl.program_id(0) * TURN + j * 128, 128), 128), :]
        out_ref[:, :, j * 128 : (j + 1) * 128] = block.T.reshape(2, 64, 128)


def shards(coeffs, interp, freq_index, target):
    f32 = jnp.float32
    anywhere = pl.BlockSpec(memory_space=pl.ANY)
    big = pltpu.VMEM((CHUNK, 128), f32)
    dma = pltpu.SemaphoreType.DMA
    positions = coeffs.shape[2]
    rows = pl.pallas_call(
        kernel,
        out_shape=jax.ShapeDtypeStruct((positions, 128), f32),
        in_specs=[pl.BlockSpec(memory_space=pltpu.HBM)] * 4,
        out_specs=anywhere,
        scratch_shapes=[
            pltpu.VMEM(coeffs.shape, f32),
            pltpu.VMEM((CHUNKS * CHUNK, 128), f32),
            big, big, big, big, big, big,
            pltpu.VMEM(interp.shape, f32),
            pltpu.VMEM(freq_index.shape, jnp.int32),
            pltpu.VMEM((16, 128), jnp.int32),
            pltpu.VMEM((16, 1, 128), f32),
            pltpu.VMEM((GROUP, 1, 128), f32),
            pltpu.VMEM((CHUNKS * CHUNK, 128), f32),
            pltpu.VMEM((24, 128), f32),
            pltpu.VMEM((128, 128), f32),
            pltpu.VMEM((9, 256, 256), jnp.bfloat16),
            pltpu.VMEM((18, CHUNKS * CHUNK, 128), f32),
            pltpu.VMEM((18, CHUNKS * CHUNK, 128), f32),
            pltpu.SemaphoreType.REGULAR((4,)),
            dma((CHUNKS,)), dma((3,)), dma((CHUNKS,)), dma, dma((4,)),
            dma((CHUNKS,)), dma((CHUNKS,)), dma((CHUNKS,)), dma((CHUNKS,)),
        ],
        compiler_params=pltpu.CompilerParams(
            collective_id=0, has_side_effects=True, vmem_limit_bytes=52 * 1024 * 1024
        ),
        name="butterfly",
    )(*(
        pltpu.with_memory_space_constraint(x, pltpu.HBM)
        for x in (coeffs, interp, freq_index, target.reshape(16, 128))
    ))
    rows = pltpu.with_memory_space_constraint(rows, pltpu.VMEM)
    return pl.pallas_call(
        turn_kernel,
        grid=(positions // TURN,),
        out_shape=jax.ShapeDtypeStruct(coeffs.shape, f32),
        in_specs=[pl.BlockSpec(memory_space=pltpu.VMEM)],
        out_specs=pl.BlockSpec((2, 64, TURN), lambda i: (0, 0, i)),
        name="turn",
    )(rows)


def solution(mesh):
    in_specs = (P(None, None, ("gx", "gy", "gz")), P(), P(), P(("gx", "gy", "gz")))
    out_specs = P(None, None, ("gx", "gy", "gz"))
    return jax.shard_map(shards, mesh=mesh, in_specs=in_specs, out_specs=out_specs, check_vma=False)
```

```python
import functools
import math

import jax
import jax.numpy as jnp
import numpy as np
from jax import lax
from jax.experimental import pallas as pl
from jax.experimental.pallas import tpu as pltpu
from jax.sharding import PartitionSpec as P

MESH = pl.DeviceIdType.MESH
GROUP = 128
PEERS = GROUP - 1
CHUNKS = 2
ROWS = 8
CHUNK = GROUP * ROWS
STEP_BITS = (6, 2, 0, 5, 3, 1, 4, 2, 0)
BLOCK = 256
TURN = 512


def turn_cos_coefficients(degree=6):
    nodes = np.cos((np.arange(400) + 0.5) * np.pi / 400)
    z = (nodes + 1) / 8
    cheb = np.polynomial.chebyshev.Chebyshev.fit(
        z, np.cos(2 * np.pi * np.sqrt(z)), degree, domain=[0, 0.25]
    )
    poly = cheb.convert(kind=np.polynomial.Polynomial, domain=[-1, 1], window=[-1, 1])
    return [float(c) for c in poly.coef]


COS = turn_cos_coefficients()


def turn_cos(r):
    x = r - jnp.round(r)
    z = x * x
    acc = jnp.full_like(z, COS[-1])
    for c in COS[-2::-1]:
        acc = acc * z + c
    return acc


def place():
    gx, gy, gz = lax.axis_index("gx"), lax.axis_index("gy"), lax.axis_index("gz")
    return gx // 8, (gx // 2) % 4, gy, gz, gx % 2


def number(xlo, z, y, g):
    return ((xlo * 4 + z) * 4 + y) * 4 + g


def plane(m):
    z = place()[1]
    return (z, z + 1 - 2 * (z % 2), (z + 2) % 4, 3 - z)[m]


def peers(*masks):
    xlo, z, y, g, low = place()
    xs = [(xlo + i) % 2 for i in range(2)]
    ys = [(y + i) % 4 for i in range(4)]
    gs = [(g + i) % 4 for i in range(4)]
    zs = {m: plane(m) for m in masks}
    out = []
    for i in range(32):
        dx, dy, dg = i // 16, i // 4 % 4, i % 4
        for m in masks:
            if m or i:
                device = (xs[dx] * 8 + zs[m] * 2 + low, ys[dy], gs[dg])
                out.append((device, number(xs[dx], zs[m], 0, 0) + ys[dy] * 4 + gs[dg]))
    return out


def all_peers():
    return peers(2) + peers(1, 3) + peers(0)


def kernel(
    coeffs_ref, interp_hbm, freq_hbm, target_hbm, rows_ref,
    x_ref, send, recv0, recv1, state0, state1, back0, back1,
    interp_ref, freq_ref, target_ref,
    tsend, trecv, turns, freqs, wide, weights, cosines, sines,
    ready, load_sem, small_sem, own_sem, tsend_sem, trecv_sem, in_send, in_recv, out_send, out_recv,
):
    xlo, z, y, g, low = place()
    me = number(xlo, z, y, g)
    recv, back = (recv0, recv1), (back0, back1)
    own = pl.ds(pl.multiple_of(me * ROWS, ROWS), ROWS)
    half = CHUNK

    def home(q, d):
        return pl.ds(pl.multiple_of((d * CHUNKS + q) * ROWS, ROWS), ROWS)

    def load(q):
        cols = pl.ds(q * half, half)
        return pltpu.make_async_copy(
            coeffs_ref.at[:, :, cols], x_ref.at[:, :, cols], load_sem.at[q]
        )

    barrier = pltpu.get_barrier_semaphore()
    above = [((xlo * 8 + plane(m) * 2 + low, y, g), m) for m in (1, 3, 2)]
    near = [device for device, _ in peers(0)] + [device for device, _ in above]
    for device in near:
        pl.semaphore_signal(barrier, inc=1, device_id=device, device_id_type=MESH)

    small = [
        pltpu.make_async_copy(src, dst, small_sem.at[i])
        for i, (src, dst) in enumerate(
            ((target_hbm, target_ref), (freq_hbm, freq_ref), (interp_hbm, interp_ref))
        )
    ]
    small[0].start()
    for q in range(CHUNKS):
        load(q).start()
    small[1].start()
    small[2].start()

    small[0].wait()
    targets = target_ref[...].astype(jnp.float32)
    for k in range(16):
        tsend[k] = targets[k : k + 1, :]

    def turn_in(q):
        load(q).wait()
        for j in range(half // 128):
            cols = slice(q * half + j * 128, q * half + (j + 1) * 128)
            block = x_ref[:, :, cols].reshape(128, 128)
            send[q * half + j * 128 : q * half + (j + 1) * 128, :] = block.T

    def copy_in(q, device, d):
        return pltpu.make_async_remote_copy(
            src_ref=send.at[home(q, d)],
            dst_ref=recv[q].at[pl.ds(pl.multiple_of(me * ROWS, ROWS), ROWS)],
            send_sem=in_send.at[q],
            recv_sem=in_recv.at[q],
            device_id=device,
            device_id_type=MESH,
        )

    def copy_out(q, device, d):
        return pltpu.make_async_remote_copy(
            src_ref=back[q].at[pl.ds(pl.multiple_of(d * ROWS, ROWS), ROWS)],
            dst_ref=rows_ref.at[home(q, me)],
            send_sem=out_send.at[q],
            recv_sem=out_recv.at[q],
            device_id=device,
            device_id_type=MESH,
        )

    def copy_target(m, device, d):
        return pltpu.make_async_remote_copy(
            src_ref=tsend.at[d // 8],
            dst_ref=trecv.at[me],
            send_sem=tsend_sem,
            recv_sem=trecv_sem.at[m],
            device_id=device,
            device_id_type=MESH,
        )

    def keep(q):
        return pltpu.make_async_copy(
            back[q].at[own],
            rows_ref.at[home(q, me)],
            own_sem.at[q],
        )

    def all_of(ref, sem):
        part = ref.at[pl.ds(0, PEERS * ROWS)]
        return pltpu.make_async_copy(part, part, sem)

    def all_targets(count, sem):
        part = trecv.at[pl.ds(0, count)]
        return pltpu.make_async_copy(part, part, sem)

    turn_in(0)
    turn_in(1)
    pl.semaphore_wait(barrier, len(near))
    for device, m in above:
        pl.semaphore_signal(ready.at[m], inc=1, device_id=device, device_id_type=MESH)
    for device, d in peers(0):
        copy_target(0, device, d).start()
    for masks in ((1, 3), (2,)):
        for m in masks:
            pl.semaphore_wait(ready.at[m], 1)
            for device, d in peers(m):
                copy_target(m, device, d).start()
        for device, d in peers(*masks):
            copy_in(0, device, d).start()
    for device, d in peers(0):
        copy_in(0, device, d).start()
    for device, d in all_peers():
        copy_in(1, device, d).start()
    for q in range(CHUNKS):
        recv[q][own, :] = send[home(q, me), :]
    trecv[me] = tsend[me // 8]

    small[1].wait()
    small[2].wait()
    for k in range(9):
        level, s = divmod(k, 3)
        for c in range(2):
            re = interp_ref[level, s, c, 0]
            im = interp_ref[level, s, c, 1]
            wide[0:64, 0:64] = re
            wide[0:64, 64:128] = -im
            wide[64:128, 0:64] = im
            wide[64:128, 64:128] = re
            w = wide[...].T
            hi = w.astype(jnp.bfloat16)
            lo = (w - hi.astype(jnp.float32)).astype(jnp.bfloat16)
            rows = slice(c * 128, (c + 1) * 128)
            weights[k, rows, 0:128] = hi
            weights[k, rows, 128:256] = lo
    for level in range(3):
        for s in range(3):
            f = freq_ref[level, s].astype(jnp.float32) * (1.0 / 1024.0)
            k = (level * 3 + s) * 2
            freqs[k : k + 2, 0:64] = f
            freqs[k : k + 2, 64:128] = f

    lane = lax.broadcasted_iota(jnp.int32, (8, 128), 1)
    row = lax.broadcasted_iota(jnp.int32, (8, 128), 0)

    def gather(q, first, count):
        mine = lane == (me % 8) * (CHUNKS * ROWS) + q * ROWS + row

        def body(i, carry):
            t = jnp.sum(jnp.where(mine, trecv[first + i], 0.0), axis=1, keepdims=True)
            rows = pl.ds(pl.multiple_of(q * half + (first + i) * 8, 8), 8)
            turns[rows, :] = jnp.broadcast_to(t, (8, 128))
            return carry

        lax.fori_loop(0, count, body, 0, unroll=8)

    lane1 = lax.broadcasted_iota(jnp.int32, (1, 128), 1)
    quarter = jnp.where(lane1 < 64, 0.0, -0.25)

    def fill(q, first, count):
        def body(i, carry):
            rows = pl.ds(pl.multiple_of(q * half + first * 8 + i * 64, 64), 64)
            t = turns[rows, :]
            low_half = lax.broadcasted_iota(jnp.int32, t.shape, 1) < 64
            for k in range(18):
                p = turn_cos(t * freqs[k : k + 1, :] + quarter)
                other = pltpu.roll(p, 64, 1)
                cosines[k, rows, :] = jnp.where(low_half, p, other)
                sines[k, rows, :] = jnp.where(low_half, -other, p)
            return carry

        lax.fori_loop(0, count // 8, body, 0)

    def mix(k, rows, child0, child1):
        rot = []
        for c, x in enumerate((child0, child1)):
            rot.append(cosines[2 * k + c, rows, :] * x + sines[2 * k + c, rows, :] * pltpu.roll(x, 64, 1))
        rot = jnp.concatenate(rot, axis=1)
        hi = rot.astype(jnp.bfloat16)
        lo = (rot - hi.astype(jnp.float32)).astype(jnp.bfloat16)
        both = jnp.dot(hi, weights[k], preferred_element_type=jnp.float32)
        rest = jnp.dot(lo, weights[k, :, 0:128], preferred_element_type=jnp.float32)
        return both[:, 0:128] + both[:, 128:256] + rest

    def step(k, q, src, dst):
        stride = ROWS << STEP_BITS[k]
        base = q * half
        if stride >= BLOCK:
            for at in range(0, half, BLOCK):
                if at & stride == 0:
                    x0 = src[at : at + BLOCK, :]
                    x1 = src[at + stride : at + stride + BLOCK, :]
                    for here in (at, at + stride):
                        dst[here : here + BLOCK, :] = mix(
                            k, slice(base + here, base + here + BLOCK), x0, x1
                        )
        else:
            for at in range(0, half, BLOCK):
                x = src[at : at + BLOCK, :].reshape(BLOCK // (2 * stride), 2, stride, 128)
                children = [
                    jnp.broadcast_to(x[:, c : c + 1], x.shape).reshape(BLOCK, 128) for c in range(2)
                ]
                dst[at : at + BLOCK, :] = mix(k, slice(base + at, base + at + BLOCK), *children)

    for m in (0, 1, 3, 2):
        all_targets(32 if m else 31, trecv_sem.at[m]).wait()

        def of_plane(x, carry, m=m):
            first = x * 64 + plane(m) * 16
            gather(0, first, 16)
            fill(0, first, 16)
            return carry

        lax.fori_loop(0, 2, of_plane, 0)
    for q in range(CHUNKS):
        all_of(recv[q], in_recv.at[q]).wait()
        states = [recv[q]] + [(state0, state1)[k % 2] for k in range(8)] + [back[q]]
        for k in range(9):
            step(k, q, states[k], states[k + 1])
        for device, d in all_peers():
            copy_out(q, device, d).start()
        keep(q).start()
        if q == 0:
            gather(1, 0, GROUP)
            fill(1, 0, GROUP)

    for q in range(CHUNKS):
        all_of(rows_ref, out_recv.at[q]).wait()
        keep(q).wait()
    all_targets(PEERS, tsend_sem).wait()
    for q in range(CHUNKS):
        all_of(send, in_send.at[q]).wait()
        all_of(back[q], out_send.at[q]).wait()


def turn_kernel(rows_ref, out_ref, y_ref, sem):
    copies = []
    for i in range(rows_ref.shape[0] // TURN):
        for j in range(i * TURN, (i + 1) * TURN, 128):
            y_ref[:, :, j : j + 128] = rows_ref[j : j + 128, :].T.reshape(2, 64, 128)
        cols = pl.ds(i * TURN, TURN)
        copies.append(pltpu.make_async_copy(y_ref.at[:, :, cols], out_ref.at[:, :, cols], sem.at[i]))
        copies[i].start()
    for copy in copies:
        copy.wait()


def shards(coeffs, interp, freq_index, target):
    f32 = jnp.float32
    anywhere = pl.BlockSpec(memory_space=pl.ANY)
    big = pltpu.VMEM((CHUNK, 128), f32)
    dma = pltpu.SemaphoreType.DMA
    positions = coeffs.shape[2]
    rows = pl.pallas_call(
        kernel,
        out_shape=jax.ShapeDtypeStruct((positions, 128), f32),
        in_specs=[pl.BlockSpec(memory_space=pltpu.HBM)] * 4,
        out_specs=anywhere,
        scratch_shapes=[
            pltpu.VMEM(coeffs.shape, f32),
            pltpu.VMEM((CHUNKS * CHUNK, 128), f32),
            big, big, big, big, big, big,
            pltpu.VMEM(interp.shape, f32),
            pltpu.VMEM(freq_index.shape, jnp.int32),
            pltpu.VMEM((16, 128), jnp.int32),
            pltpu.VMEM((16, 1, 128), f32),
            pltpu.VMEM((GROUP, 1, 128), f32),
            pltpu.VMEM((CHUNKS * CHUNK, 128), f32),
            pltpu.VMEM((24, 128), f32),
            pltpu.VMEM((128, 128), f32),
            pltpu.VMEM((9, 256, 256), jnp.bfloat16),
            pltpu.VMEM((18, CHUNKS * CHUNK, 128), f32),
            pltpu.VMEM((18, CHUNKS * CHUNK, 128), f32),
            pltpu.SemaphoreType.REGULAR((4,)),
            dma((CHUNKS,)), dma((3,)), dma((CHUNKS,)), dma, dma((4,)),
            dma((CHUNKS,)), dma((CHUNKS,)), dma((CHUNKS,)), dma((CHUNKS,)),
        ],
        compiler_params=pltpu.CompilerParams(
            collective_id=0, has_side_effects=True, vmem_limit_bytes=52 * 1024 * 1024
        ),
        name="butterfly",
    )(*(
        pltpu.with_memory_space_constraint(x, pltpu.HBM)
        for x in (coeffs, interp, freq_index, target.reshape(16, 128))
    ))
    rows = pltpu.with_memory_space_constraint(rows, pltpu.VMEM)
    return pl.pallas_call(
        turn_kernel,
        out_shape=jax.ShapeDtypeStruct(coeffs.shape, f32),
        in_specs=[pl.BlockSpec(memory_space=pltpu.VMEM)],
        out_specs=pl.BlockSpec(memory_space=pltpu.HBM),
        scratch_shapes=[pltpu.VMEM(coeffs.shape, f32), dma((positions // TURN,))],
        name="turn",
    )(rows)


def solution(mesh):
    in_specs = (P(None, None, ("gx", "gy", "gz")), P(), P(), P(("gx", "gy", "gz")))
    out_specs = P(None, None, ("gx", "gy", "gz"))
    return jax.shard_map(shards, mesh=mesh, in_specs=in_specs, out_specs=out_specs, check_vma=False)
```

```python
import functools
import math

import jax
import jax.numpy as jnp
import numpy as np
from jax import lax
from jax.experimental import pallas as pl
from jax.experimental.pallas import tpu as pltpu
from jax.sharding import PartitionSpec as P

MESH = pl.DeviceIdType.MESH
GROUP = 128
PEERS = GROUP - 1
CHUNKS = 2
ROWS = 8
CHUNK = GROUP * ROWS
STEP_BITS = (6, 2, 0, 5, 3, 1, 4, 2, 0)
BLOCK = 256
TURN = 512


def turn_cos_coefficients(degree=6):
    nodes = np.cos((np.arange(400) + 0.5) * np.pi / 400)
    z = (nodes + 1) / 8
    cheb = np.polynomial.chebyshev.Chebyshev.fit(
        z, np.cos(2 * np.pi * np.sqrt(z)), degree, domain=[0, 0.25]
    )
    poly = cheb.convert(kind=np.polynomial.Polynomial, domain=[-1, 1], window=[-1, 1])
    return [float(c) for c in poly.coef]


COS = turn_cos_coefficients()


def turn_cos(r):
    x = r - jnp.round(r)
    z = x * x
    acc = jnp.full_like(z, COS[-1])
    for c in COS[-2::-1]:
        acc = acc * z + c
    return acc


def place():
    gx, gy, gz = lax.axis_index("gx"), lax.axis_index("gy"), lax.axis_index("gz")
    return gx // 8, (gx // 2) % 4, gy, gz, gx % 2


def number(xlo, z, y, g):
    return ((xlo * 4 + z) * 4 + y) * 4 + g


def plane(dz):
    return (place()[1] + dz) % 4


def peers(*steps):
    xlo, z, y, g, low = place()
    xs = [(xlo + i) % 2 for i in range(2)]
    ys = [(y + i) % 4 for i in range(4)]
    gs = [(g + i) % 4 for i in range(4)]
    zs = {dz: plane(dz) for dz in steps}
    out = []
    for i in range(32):
        dx, dy, dg = i // 16, i // 4 % 4, i % 4
        for dz in steps:
            if dz or i:
                device = (xs[dx] * 8 + zs[dz] * 2 + low, ys[dy], gs[dg])
                out.append((device, number(xs[dx], zs[dz], 0, 0) + ys[dy] * 4 + gs[dg]))
    return out


def all_peers():
    return peers(2) + peers(1, 3) + peers(0)


def kernel(
    coeffs_ref, interp_hbm, freq_hbm, target_hbm, rows_ref,
    x_ref, send, recv0, recv1, state0, state1, back0, back1,
    interp_ref, freq_ref, target_ref,
    tsend, trecv, turns, freqs, wide, weights, cosines, sines,
    ready, load_sem, small_sem, own_sem, tsend_sem, trecv_sem, in_send, in_recv, out_send, out_recv,
):
    xlo, z, y, g, low = place()
    me = number(xlo, z, y, g)
    recv, back = (recv0, recv1), (back0, back1)
    own = pl.ds(pl.multiple_of(me * ROWS, ROWS), ROWS)
    half = CHUNK

    def home(q, d):
        return pl.ds(pl.multiple_of((d * CHUNKS + q) * ROWS, ROWS), ROWS)

    def load(q):
        cols = pl.ds(q * half, half)
        return pltpu.make_async_copy(
            coeffs_ref.at[:, :, cols], x_ref.at[:, :, cols], load_sem.at[q]
        )

    barrier = pltpu.get_barrier_semaphore()
    above = [((xlo * 8 + plane(dz) * 2 + low, y, g), dz) for dz in (2, 1, 3)]
    near = [device for device, _ in peers(0)] + [device for device, _ in above]
    for device in near:
        pl.semaphore_signal(barrier, inc=1, device_id=device, device_id_type=MESH)

    small = [
        pltpu.make_async_copy(src, dst, small_sem.at[i])
        for i, (src, dst) in enumerate(
            ((target_hbm, target_ref), (freq_hbm, freq_ref), (interp_hbm, interp_ref))
        )
    ]
    small[0].start()
    for q in range(CHUNKS):
        load(q).start()
    small[1].start()
    small[2].start()

    small[0].wait()
    targets = target_ref[...].astype(jnp.float32)
    for k in range(16):
        tsend[k] = targets[k : k + 1, :]

    def turn_in(q):
        load(q).wait()
        for j in range(half // 128):
            cols = slice(q * half + j * 128, q * half + (j + 1) * 128)
            block = x_ref[:, :, cols].reshape(128, 128)
            send[q * half + j * 128 : q * half + (j + 1) * 128, :] = block.T

    def copy_in(q, device, d):
        return pltpu.make_async_remote_copy(
            src_ref=send.at[home(q, d)],
            dst_ref=recv[q].at[pl.ds(pl.multiple_of(me * ROWS, ROWS), ROWS)],
            send_sem=in_send.at[q],
            recv_sem=in_recv.at[q],
            device_id=device,
            device_id_type=MESH,
        )

    def copy_out(q, device, d):
        return pltpu.make_async_remote_copy(
            src_ref=back[q].at[pl.ds(pl.multiple_of(d * ROWS, ROWS), ROWS)],
            dst_ref=rows_ref.at[home(q, me)],
            send_sem=out_send.at[q],
            recv_sem=out_recv.at[q],
            device_id=device,
            device_id_type=MESH,
        )

    def copy_target(dz, device, d):
        return pltpu.make_async_remote_copy(
            src_ref=tsend.at[d // 8],
            dst_ref=trecv.at[me],
            send_sem=tsend_sem,
            recv_sem=trecv_sem.at[(4 - dz) % 4],
            device_id=device,
            device_id_type=MESH,
        )

    def keep(q):
        return pltpu.make_async_copy(
            back[q].at[own],
            rows_ref.at[home(q, me)],
            own_sem.at[q],
        )

    def all_of(ref, sem):
        part = ref.at[pl.ds(0, PEERS * ROWS)]
        return pltpu.make_async_copy(part, part, sem)

    def all_targets(count, sem):
        part = trecv.at[pl.ds(0, count)]
        return pltpu.make_async_copy(part, part, sem)

    turn_in(0)
    turn_in(1)
    pl.semaphore_wait(barrier, len(near))
    for device, dz in above:
        pl.semaphore_signal(ready.at[4 - dz], inc=1, device_id=device, device_id_type=MESH)
    for dz in (0, 1, 3, 2):
        if dz:
            pl.semaphore_wait(ready.at[dz], 1)
        for device, d in peers(dz):
            copy_target(dz, device, d).start()
    for device, d in all_peers():
        copy_in(0, device, d).start()
    for device, d in all_peers():
        copy_in(1, device, d).start()
    for q in range(CHUNKS):
        recv[q][own, :] = send[home(q, me), :]
    trecv[me] = tsend[me // 8]

    small[1].wait()
    small[2].wait()
    for k in range(9):
        level, s = divmod(k, 3)
        for c in range(2):
            re = interp_ref[level, s, c, 0]
            im = interp_ref[level, s, c, 1]
            wide[0:64, 0:64] = re
            wide[0:64, 64:128] = -im
            wide[64:128, 0:64] = im
            wide[64:128, 64:128] = re
            w = wide[...].T
            hi = w.astype(jnp.bfloat16)
            lo = (w - hi.astype(jnp.float32)).astype(jnp.bfloat16)
            rows = slice(c * 128, (c + 1) * 128)
            weights[k, rows, 0:128] = hi
            weights[k, rows, 128:256] = lo
    for level in range(3):
        for s in range(3):
            f = freq_ref[level, s].astype(jnp.float32) * (1.0 / 1024.0)
            k = (level * 3 + s) * 2
            freqs[k : k + 2, 0:64] = f
            freqs[k : k + 2, 64:128] = f

    lane = lax.broadcasted_iota(jnp.int32, (8, 128), 1)
    row = lax.broadcasted_iota(jnp.int32, (8, 128), 0)

    def gather(q, first, count):
        mine = lane == (me % 8) * (CHUNKS * ROWS) + q * ROWS + row

        def body(i, carry):
            t = jnp.sum(jnp.where(mine, trecv[first + i], 0.0), axis=1, keepdims=True)
            rows = pl.ds(pl.multiple_of(q * half + (first + i) * 8, 8), 8)
            turns[rows, :] = jnp.broadcast_to(t, (8, 128))
            return carry

        lax.fori_loop(0, count, body, 0, unroll=8)

    lane1 = lax.broadcasted_iota(jnp.int32, (1, 128), 1)
    quarter = jnp.where(lane1 < 64, 0.0, -0.25)

    def fill(q, first, count):
        def body(i, carry):
            rows = pl.ds(pl.multiple_of(q * half + first * 8 + i * 64, 64), 64)
            t = turns[rows, :]
            low_half = lax.broadcasted_iota(jnp.int32, t.shape, 1) < 64
            for k in range(18):
                p = turn_cos(t * freqs[k : k + 1, :] + quarter)
                other = pltpu.roll(p, 64, 1)
                cosines[k, rows, :] = jnp.where(low_half, p, other)
                sines[k, rows, :] = jnp.where(low_half, -other, p)
            return carry

        lax.fori_loop(0, count // 8, body, 0)

    def mix(k, rows, child0, child1):
        rot = []
        for c, x in enumerate((child0, child1)):
            rot.append(cosines[2 * k + c, rows, :] * x + sines[2 * k + c, rows, :] * pltpu.roll(x, 64, 1))
        rot = jnp.concatenate(rot, axis=1)
        hi = rot.astype(jnp.bfloat16)
        lo = (rot - hi.astype(jnp.float32)).astype(jnp.bfloat16)
        both = jnp.dot(hi, weights[k], preferred_element_type=jnp.float32)
        rest = jnp.dot(lo, weights[k, :, 0:128], preferred_element_type=jnp.float32)
        return both[:, 0:128] + both[:, 128:256] + rest

    def step(k, q, src, dst):
        stride = ROWS << STEP_BITS[k]
        base = q * half
        if stride >= BLOCK:
            for at in range(0, half, BLOCK):
                if at & stride == 0:
                    x0 = src[at : at + BLOCK, :]
                    x1 = src[at + stride : at + stride + BLOCK, :]
                    for here in (at, at + stride):
                        dst[here : here + BLOCK, :] = mix(
                            k, slice(base + here, base + here + BLOCK), x0, x1
                        )
        else:
            for at in range(0, half, BLOCK):
                x = src[at : at + BLOCK, :].reshape(BLOCK // (2 * stride), 2, stride, 128)
                children = [
                    jnp.broadcast_to(x[:, c : c + 1], x.shape).reshape(BLOCK, 128) for c in range(2)
                ]
                dst[at : at + BLOCK, :] = mix(k, slice(base + at, base + at + BLOCK), *children)

    for dz in (0, 1, 3, 2):
        all_targets(32 if dz else 31, trecv_sem.at[dz]).wait()

        def of_plane(x, carry, dz=dz):
            first = x * 64 + plane(dz) * 16
            gather(0, first, 16)
            fill(0, first, 16)
            return carry

        lax.fori_loop(0, 2, of_plane, 0)
    for q in range(CHUNKS):
        all_of(recv[q], in_recv.at[q]).wait()
        states = [recv[q]] + [(state0, state1)[k % 2] for k in range(8)] + [back[q]]
        for k in range(9):
            step(k, q, states[k], states[k + 1])
        for device, d in all_peers():
            copy_out(q, device, d).start()
        keep(q).start()
        if q == 0:
            gather(1, 0, GROUP)
            fill(1, 0, GROUP)

    for q in range(CHUNKS):
        all_of(rows_ref, out_recv.at[q]).wait()
        keep(q).wait()
    all_targets(PEERS, tsend_sem).wait()
    for q in range(CHUNKS):
        all_of(send, in_send.at[q]).wait()
        all_of(back[q], out_send.at[q]).wait()


def turn_kernel(rows_ref, out_ref, y_ref, sem):
    copies = []
    for i in range(rows_ref.shape[0] // TURN):
        for j in range(i * TURN, (i + 1) * TURN, 128):
            y_ref[:, :, j : j + 128] = rows_ref[j : j + 128, :].T.reshape(2, 64, 128)
        cols = pl.ds(i * TURN, TURN)
        copies.append(pltpu.make_async_copy(y_ref.at[:, :, cols], out_ref.at[:, :, cols], sem.at[i]))
        copies[i].start()
    for copy in copies:
        copy.wait()


def shards(coeffs, interp, freq_index, target):
    f32 = jnp.float32
    anywhere = pl.BlockSpec(memory_space=pl.ANY)
    big = pltpu.VMEM((CHUNK, 128), f32)
    dma = pltpu.SemaphoreType.DMA
    positions = coeffs.shape[2]
    rows = pl.pallas_call(
        kernel,
        out_shape=jax.ShapeDtypeStruct((positions, 128), f32),
        in_specs=[pl.BlockSpec(memory_space=pltpu.HBM)] * 4,
        out_specs=anywhere,
        scratch_shapes=[
            pltpu.VMEM(coeffs.shape, f32),
            pltpu.VMEM((CHUNKS * CHUNK, 128), f32),
            big, big, big, big, big, big,
            pltpu.VMEM(interp.shape, f32),
            pltpu.VMEM(freq_index.shape, jnp.int32),
            pltpu.VMEM((16, 128), jnp.int32),
            pltpu.VMEM((16, 1, 128), f32),
            pltpu.VMEM((GROUP, 1, 128), f32),
            pltpu.VMEM((CHUNKS * CHUNK, 128), f32),
            pltpu.VMEM((24, 128), f32),
            pltpu.VMEM((128, 128), f32),
            pltpu.VMEM((9, 256, 256), jnp.bfloat16),
            pltpu.VMEM((18, CHUNKS * CHUNK, 128), f32),
            pltpu.VMEM((18, CHUNKS * CHUNK, 128), f32),
            pltpu.SemaphoreType.REGULAR((4,)),
            dma((CHUNKS,)), dma((3,)), dma((CHUNKS,)), dma, dma((4,)),
            dma((CHUNKS,)), dma((CHUNKS,)), dma((CHUNKS,)), dma((CHUNKS,)),
        ],
        compiler_params=pltpu.CompilerParams(
            collective_id=0, has_side_effects=True, vmem_limit_bytes=52 * 1024 * 1024
        ),
        name="butterfly",
    )(*(
        pltpu.with_memory_space_constraint(x, pltpu.HBM)
        for x in (coeffs, interp, freq_index, target.reshape(16, 128))
    ))
    rows = pltpu.with_memory_space_constraint(rows, pltpu.VMEM)
    return pl.pallas_call(
        turn_kernel,
        out_shape=jax.ShapeDtypeStruct(coeffs.shape, f32),
        in_specs=[pl.BlockSpec(memory_space=pltpu.VMEM)],
        out_specs=pl.BlockSpec(memory_space=pltpu.HBM),
        scratch_shapes=[pltpu.VMEM(coeffs.shape, f32), dma((positions // TURN,))],
        name="turn",
    )(rows)


def solution(mesh):
    in_specs = (P(None, None, ("gx", "gy", "gz")), P(), P(), P(("gx", "gy", "gz")))
    out_specs = P(None, None, ("gx", "gy", "gz"))
    return jax.shard_map(shards, mesh=mesh, in_specs=in_specs, out_specs=out_specs, check_vma=False)
```

```python
import functools
import math

import jax
import jax.numpy as jnp
import numpy as np
from jax import lax
from jax.experimental import pallas as pl
from jax.experimental.pallas import tpu as pltpu
from jax.sharding import PartitionSpec as P

MESH = pl.DeviceIdType.MESH
GROUP = 128
PEERS = GROUP - 1
CHUNKS = 2
ROWS = 8
CHUNK = GROUP * ROWS
STEP_BITS = (6, 2, 0, 5, 3, 1, 4, 2, 0)
BLOCK = 256
TURN = 512


def turn_cos_coefficients(degree=6):
    nodes = np.cos((np.arange(400) + 0.5) * np.pi / 400)
    z = (nodes + 1) / 8
    cheb = np.polynomial.chebyshev.Chebyshev.fit(
        z, np.cos(2 * np.pi * np.sqrt(z)), degree, domain=[0, 0.25]
    )
    poly = cheb.convert(kind=np.polynomial.Polynomial, domain=[-1, 1], window=[-1, 1])
    return [float(c) for c in poly.coef]


COS = turn_cos_coefficients()


def turn_cos(r):
    x = r - jnp.round(r)
    z = x * x
    acc = jnp.full_like(z, COS[-1])
    for c in COS[-2::-1]:
        acc = acc * z + c
    return acc


def place():
    gx, gy, gz = lax.axis_index("gx"), lax.axis_index("gy"), lax.axis_index("gz")
    return gx // 8, (gx // 2) % 4, gy, gz, gx % 2


def number(xlo, z, y, g):
    return ((xlo * 4 + z) * 4 + y) * 4 + g


AWAY_FIRST = ((2,), (1, 3), (0,))
IN_TURN = ((2, 1, 0, 3),)


def each_peer(fn, order=AWAY_FIRST):
    xlo, z, y, g, low = place()
    xs = [(xlo + i) % 2 for i in range(2)]
    zs = [(z + i) % 4 for i in range(4)]
    ys = [(y + i) % 4 for i in range(4)]
    gs = [(g + i) % 4 for i in range(4)]
    for dzs in order:
        for dx in range(2):
            for dy in range(4):
                for dg in range(4):
                    for dz in dzs:
                        if dz or dx or dy or dg:
                            gx = xs[dx] * 8 + zs[dz] * 2 + low
                            first = number(xs[dx], zs[dz], 0, 0)
                            fn((gx, ys[dy], gs[dg]), first + ys[dy] * 4 + gs[dg])


def kernel(
    coeffs_ref, interp_hbm, freq_hbm, target_hbm, rows_ref,
    x_ref, send, recv0, recv1, state0, state1, back0, back1,
    interp_ref, freq_ref, target_ref,
    tsend, trecv, turns, freqs, wide, weights, cosines, sines,
    load_sem, small_sem, own_sem, tsend_sem, trecv_sem, in_send, in_recv, out_send, out_recv,
):
    xlo, z, y, g, low = place()
    me = number(xlo, z, y, g)
    recv, back = (recv0, recv1), (back0, back1)
    own = pl.ds(pl.multiple_of(me * ROWS, ROWS), ROWS)
    half = CHUNK

    def home(q, d):
        return pl.ds(pl.multiple_of((d * CHUNKS + q) * ROWS, ROWS), ROWS)

    def load(q):
        cols = pl.ds(q * half, half)
        return pltpu.make_async_copy(
            coeffs_ref.at[:, :, cols], x_ref.at[:, :, cols], load_sem.at[q]
        )

    barrier = pltpu.get_barrier_semaphore()
    each_peer(
        lambda device, d: pl.semaphore_signal(
            barrier, inc=1, device_id=device, device_id_type=MESH
        )
    )

    small = [
        pltpu.make_async_copy(src, dst, small_sem.at[i])
        for i, (src, dst) in enumerate(
            ((target_hbm, target_ref), (freq_hbm, freq_ref), (interp_hbm, interp_ref))
        )
    ]
    small[0].start()
    for q in range(CHUNKS):
        load(q).start()
    small[1].start()
    small[2].start()

    small[0].wait()
    targets = target_ref[...].astype(jnp.float32)
    for k in range(16):
        tsend[k] = targets[k : k + 1, :]

    def turn_in(q):
        load(q).wait()
        for j in range(half // 128):
            cols = slice(q * half + j * 128, q * half + (j + 1) * 128)
            block = x_ref[:, :, cols].reshape(128, 128)
            send[q * half + j * 128 : q * half + (j + 1) * 128, :] = block.T

    def copy_in(q, device, d):
        return pltpu.make_async_remote_copy(
            src_ref=send.at[home(q, d)],
            dst_ref=recv[q].at[pl.ds(pl.multiple_of(me * ROWS, ROWS), ROWS)],
            send_sem=in_send.at[q],
            recv_sem=in_recv.at[q],
            device_id=device,
            device_id_type=MESH,
        )

    def copy_out(q, device, d):
        return pltpu.make_async_remote_copy(
            src_ref=back[q].at[pl.ds(pl.multiple_of(d * ROWS, ROWS), ROWS)],
            dst_ref=rows_ref.at[home(q, me)],
            send_sem=out_send.at[q],
            recv_sem=out_recv.at[q],
            device_id=device,
            device_id_type=MESH,
        )

    def copy_target(device, d):
        return pltpu.make_async_remote_copy(
            src_ref=tsend.at[d // 8],
            dst_ref=trecv.at[me],
            send_sem=tsend_sem,
            recv_sem=trecv_sem,
            device_id=device,
            device_id_type=MESH,
        )

    def keep(q):
        return pltpu.make_async_copy(
            back[q].at[own],
            rows_ref.at[home(q, me)],
            own_sem.at[q],
        )

    def all_of(ref, sem):
        part = ref.at[pl.ds(0, PEERS * ROWS)]
        return pltpu.make_async_copy(part, part, sem)

    def all_targets(sem):
        part = trecv.at[pl.ds(0, PEERS)]
        return pltpu.make_async_copy(part, part, sem)

    turn_in(0)
    turn_in(1)
    pl.semaphore_wait(barrier, PEERS)
    each_peer(lambda device, d: copy_target(device, d).start())
    each_peer(lambda device, d: copy_in(0, device, d).start(), IN_TURN)
    each_peer(lambda device, d: copy_in(1, device, d).start(), IN_TURN)
    for q in range(CHUNKS):
        recv[q][own, :] = send[home(q, me), :]
    trecv[me] = tsend[me // 8]

    small[1].wait()
    small[2].wait()
    for k in range(9):
        level, s = divmod(k, 3)
        for c in range(2):
            re = interp_ref[level, s, c, 0]
            im = interp_ref[level, s, c, 1]
            wide[0:64, 0:64] = re
            wide[0:64, 64:128] = -im
            wide[64:128, 0:64] = im
            wide[64:128, 64:128] = re
            w = wide[...].T
            hi = w.astype(jnp.bfloat16)
            lo = (w - hi.astype(jnp.float32)).astype(jnp.bfloat16)
            rows = slice(c * 128, (c + 1) * 128)
            weights[k, rows, 0:128] = hi
            weights[k, rows, 128:256] = lo
    for level in range(3):
        for s in range(3):
            f = freq_ref[level, s].astype(jnp.float32) * (1.0 / 1024.0)
            k = (level * 3 + s) * 2
            freqs[k : k + 2, 0:64] = f
            freqs[k : k + 2, 64:128] = f

    lane = lax.broadcasted_iota(jnp.int32, (8, 128), 1)
    row = lax.broadcasted_iota(jnp.int32, (8, 128), 0)
    all_targets(trecv_sem).wait()
    for q in range(CHUNKS):

        mine = lane == (me % 8) * (CHUNKS * ROWS) + q * ROWS + row

        def gather(i, carry, q=q, mine=mine):
            t = trecv[i]
            t = jnp.sum(jnp.where(mine, t, 0.0), axis=1, keepdims=True)
            turns[pl.ds(pl.multiple_of(q * half + i * 8, 8), 8), :] = jnp.broadcast_to(t, (8, 128))
            return carry

        lax.fori_loop(0, GROUP, gather, 0, unroll=8)

    lane1 = lax.broadcasted_iota(jnp.int32, (1, 128), 1)
    quarter = jnp.where(lane1 < 64, 0.0, -0.25)

    def fill(q, first, last):
        def body(i, carry):
            rows = pl.ds(pl.multiple_of(q * half + i * 64, 64), 64)
            t = turns[rows, :]
            low_half = lax.broadcasted_iota(jnp.int32, t.shape, 1) < 64
            for k in range(18):
                p = turn_cos(t * freqs[k : k + 1, :] + quarter)
                other = pltpu.roll(p, 64, 1)
                cosines[k, rows, :] = jnp.where(low_half, p, other)
                sines[k, rows, :] = jnp.where(low_half, -other, p)
            return carry

        lax.fori_loop(first, last, body, 0)

    def mix(k, rows, child0, child1):
        rot = []
        for c, x in enumerate((child0, child1)):
            rot.append(cosines[2 * k + c, rows, :] * x + sines[2 * k + c, rows, :] * pltpu.roll(x, 64, 1))
        rot = jnp.concatenate(rot, axis=1)
        hi = rot.astype(jnp.bfloat16)
        lo = (rot - hi.astype(jnp.float32)).astype(jnp.bfloat16)
        both = jnp.dot(hi, weights[k], preferred_element_type=jnp.float32)
        rest = jnp.dot(lo, weights[k, :, 0:128], preferred_element_type=jnp.float32)
        return both[:, 0:128] + both[:, 128:256] + rest

    def step(k, q, src, dst):
        stride = ROWS << STEP_BITS[k]
        base = q * half
        if stride >= BLOCK:
            for at in range(0, half, BLOCK):
                if at & stride == 0:
                    x0 = src[at : at + BLOCK, :]
                    x1 = src[at + stride : at + stride + BLOCK, :]
                    for here in (at, at + stride):
                        dst[here : here + BLOCK, :] = mix(
                            k, slice(base + here, base + here + BLOCK), x0, x1
                        )
        else:
            for at in range(0, half, BLOCK):
                x = src[at : at + BLOCK, :].reshape(BLOCK // (2 * stride), 2, stride, 128)
                children = [
                    jnp.broadcast_to(x[:, c : c + 1], x.shape).reshape(BLOCK, 128) for c in range(2)
                ]
                dst[at : at + BLOCK, :] = mix(k, slice(base + at, base + at + BLOCK), *children)

    fill(0, 0, half // 64)
    for q in range(CHUNKS):
        all_of(recv[q], in_recv.at[q]).wait()
        states = [recv[q]] + [(state0, state1)[k % 2] for k in range(8)] + [back[q]]
        for k in range(9):
            step(k, q, states[k], states[k + 1])
        each_peer(
            lambda device, d, q=q: copy_out(q, device, d).start(), AWAY_FIRST if q else IN_TURN
        )
        keep(q).start()
        if q == 0:
            fill(1, 0, half // 64)

    for q in range(CHUNKS):
        all_of(rows_ref, out_recv.at[q]).wait()
        keep(q).wait()
    all_targets(tsend_sem).wait()
    for q in range(CHUNKS):
        all_of(send, in_send.at[q]).wait()
        all_of(back[q], out_send.at[q]).wait()


def turn_kernel(rows_ref, out_ref, y_ref, sem):
    copies = []
    for i in range(rows_ref.shape[0] // TURN):
        for j in range(i * TURN, (i + 1) * TURN, 128):
            y_ref[:, :, j : j + 128] = rows_ref[j : j + 128, :].T.reshape(2, 64, 128)
        cols = pl.ds(i * TURN, TURN)
        copies.append(pltpu.make_async_copy(y_ref.at[:, :, cols], out_ref.at[:, :, cols], sem.at[i]))
        copies[i].start()
    for copy in copies:
        copy.wait()


def shards(coeffs, interp, freq_index, target):
    f32 = jnp.float32
    anywhere = pl.BlockSpec(memory_space=pl.ANY)
    big = pltpu.VMEM((CHUNK, 128), f32)
    dma = pltpu.SemaphoreType.DMA
    positions = coeffs.shape[2]
    rows = pl.pallas_call(
        kernel,
        out_shape=jax.ShapeDtypeStruct((positions, 128), f32),
        in_specs=[pl.BlockSpec(memory_space=pltpu.HBM)] * 4,
        out_specs=anywhere,
        scratch_shapes=[
            pltpu.VMEM(coeffs.shape, f32),
            pltpu.VMEM((CHUNKS * CHUNK, 128), f32),
            big, big, big, big, big, big,
            pltpu.VMEM(interp.shape, f32),
            pltpu.VMEM(freq_index.shape, jnp.int32),
            pltpu.VMEM((16, 128), jnp.int32),
            pltpu.VMEM((16, 1, 128), f32),
            pltpu.VMEM((GROUP, 1, 128), f32),
            pltpu.VMEM((CHUNKS * CHUNK, 128), f32),
            pltpu.VMEM((24, 128), f32),
            pltpu.VMEM((128, 128), f32),
            pltpu.VMEM((9, 256, 256), jnp.bfloat16),
            pltpu.VMEM((18, CHUNKS * CHUNK, 128), f32),
            pltpu.VMEM((18, CHUNKS * CHUNK, 128), f32),
            dma((CHUNKS,)), dma((3,)), dma((CHUNKS,)), dma, dma,
            dma((CHUNKS,)), dma((CHUNKS,)), dma((CHUNKS,)), dma((CHUNKS,)),
        ],
        compiler_params=pltpu.CompilerParams(
            collective_id=0, has_side_effects=True, vmem_limit_bytes=52 * 1024 * 1024
        ),
        name="butterfly",
    )(*(
        pltpu.with_memory_space_constraint(x, pltpu.HBM)
        for x in (coeffs, interp, freq_index, target.reshape(16, 128))
    ))
    rows = pltpu.with_memory_space_constraint(rows, pltpu.VMEM)
    return pl.pallas_call(
        turn_kernel,
        out_shape=jax.ShapeDtypeStruct(coeffs.shape, f32),
        in_specs=[pl.BlockSpec(memory_space=pltpu.VMEM)],
        out_specs=pl.BlockSpec(memory_space=pltpu.HBM),
        scratch_shapes=[pltpu.VMEM(coeffs.shape, f32), dma((positions // TURN,))],
        name="turn",
    )(rows)


def solution(mesh):
    in_specs = (P(None, None, ("gx", "gy", "gz")), P(), P(), P(("gx", "gy", "gz")))
    out_specs = P(None, None, ("gx", "gy", "gz"))
    return jax.shard_map(shards, mesh=mesh, in_specs=in_specs, out_specs=out_specs, check_vma=False)
```

```python
import functools
import math

import jax
import jax.numpy as jnp
import numpy as np
from jax import lax
from jax.experimental import pallas as pl
from jax.experimental.pallas import tpu as pltpu
from jax.sharding import PartitionSpec as P

MESH = pl.DeviceIdType.MESH
GROUP = 128
PEERS = GROUP - 1
CHUNKS = 2
ROWS = 8
CHUNK = GROUP * ROWS
STEP_BITS = (6, 2, 0, 5, 3, 1, 4, 2, 0)
BLOCK = 256
TURN = 512


def turn_cos_coefficients(degree=6):
    nodes = np.cos((np.arange(400) + 0.5) * np.pi / 400)
    z = (nodes + 1) / 8
    cheb = np.polynomial.chebyshev.Chebyshev.fit(
        z, np.cos(2 * np.pi * np.sqrt(z)), degree, domain=[0, 0.25]
    )
    poly = cheb.convert(kind=np.polynomial.Polynomial, domain=[-1, 1], window=[-1, 1])
    return [float(c) for c in poly.coef]


COS = turn_cos_coefficients()


def turn_cos(r):
    x = r - jnp.round(r)
    z = x * x
    acc = jnp.full_like(z, COS[-1])
    for c in COS[-2::-1]:
        acc = acc * z + c
    return acc


def place():
    gx, gy, gz = lax.axis_index("gx"), lax.axis_index("gy"), lax.axis_index("gz")
    return gx // 8, (gx // 2) % 4, gy, gz, gx % 2


def number(xlo, z, y, g):
    return ((xlo * 4 + z) * 4 + y) * 4 + g


AWAY_FIRST = ((2,), (1, 3), (0,))
IN_TURN = ((2, 1, 0, 3),)


def each_peer(fn, order=AWAY_FIRST):
    xlo, z, y, g, low = place()
    xs = [(xlo + i) % 2 for i in range(2)]
    zs = [(z + i) % 4 for i in range(4)]
    ys = [(y + i) % 4 for i in range(4)]
    gs = [(g + i) % 4 for i in range(4)]
    for dzs in order:
        for dx in range(2):
            for dy in range(4):
                for dg in range(4):
                    for dz in dzs:
                        if dz or dx or dy or dg:
                            gx = xs[dx] * 8 + zs[dz] * 2 + low
                            first = number(xs[dx], zs[dz], 0, 0)
                            fn((gx, ys[dy], gs[dg]), first + ys[dy] * 4 + gs[dg])


def kernel(
    coeffs_ref, interp_hbm, freq_hbm, target_hbm, rows_ref,
    x_ref, send, recv0, recv1, state0, state1, back0, back1,
    interp_ref, freq_ref, target_ref,
    tsend, trecv, turns, freqs, wide, weights, cosines, sines,
    ready, load_sem, small_sem, own_sem, tsend_sem, trecv_sem, in_send, in_recv, out_send, out_recv,
):
    xlo, z, y, g, low = place()
    me = number(xlo, z, y, g)
    recv, back = (recv0, recv1), (back0, back1)
    own = pl.ds(pl.multiple_of(me * ROWS, ROWS), ROWS)
    half = CHUNK

    def home(q, d):
        return pl.ds(pl.multiple_of((d * CHUNKS + q) * ROWS, ROWS), ROWS)

    def load(q):
        cols = pl.ds(q * half, half)
        return pltpu.make_async_copy(
            coeffs_ref.at[:, :, cols], x_ref.at[:, :, cols], load_sem.at[q]
        )

    barrier = pltpu.get_barrier_semaphore()
    above = [((xlo * 8 + (z + dz) % 4 * 2 + low, y, g), dz) for dz in (2, 1, 3)]
    near = [device for device, _ in above]
    each_peer(lambda device, d: near.append(device), ((0,),))
    for device in near:
        pl.semaphore_signal(barrier, inc=1, device_id=device, device_id_type=MESH)

    small = [
        pltpu.make_async_copy(src, dst, small_sem.at[i])
        for i, (src, dst) in enumerate(
            ((target_hbm, target_ref), (freq_hbm, freq_ref), (interp_hbm, interp_ref))
        )
    ]
    small[0].start()
    for q in range(CHUNKS):
        load(q).start()
    small[1].start()
    small[2].start()

    small[0].wait()
    targets = target_ref[...].astype(jnp.float32)
    for k in range(16):
        tsend[k] = targets[k : k + 1, :]

    def turn_in(q):
        load(q).wait()
        for j in range(half // 128):
            cols = slice(q * half + j * 128, q * half + (j + 1) * 128)
            block = x_ref[:, :, cols].reshape(128, 128)
            send[q * half + j * 128 : q * half + (j + 1) * 128, :] = block.T

    def copy_in(q, device, d):
        return pltpu.make_async_remote_copy(
            src_ref=send.at[home(q, d)],
            dst_ref=recv[q].at[pl.ds(pl.multiple_of(me * ROWS, ROWS), ROWS)],
            send_sem=in_send.at[q],
            recv_sem=in_recv.at[q],
            device_id=device,
            device_id_type=MESH,
        )

    def copy_out(q, device, d):
        return pltpu.make_async_remote_copy(
            src_ref=back[q].at[pl.ds(pl.multiple_of(d * ROWS, ROWS), ROWS)],
            dst_ref=rows_ref.at[home(q, me)],
            send_sem=out_send.at[q],
            recv_sem=out_recv.at[q],
            device_id=device,
            device_id_type=MESH,
        )

    def copy_target(device, d):
        return pltpu.make_async_remote_copy(
            src_ref=tsend.at[d // 8],
            dst_ref=trecv.at[me],
            send_sem=tsend_sem,
            recv_sem=trecv_sem,
            device_id=device,
            device_id_type=MESH,
        )

    def keep(q):
        return pltpu.make_async_copy(
            back[q].at[own],
            rows_ref.at[home(q, me)],
            own_sem.at[q],
        )

    def all_of(ref, sem):
        part = ref.at[pl.ds(0, PEERS * ROWS)]
        return pltpu.make_async_copy(part, part, sem)

    def all_targets(sem):
        part = trecv.at[pl.ds(0, PEERS)]
        return pltpu.make_async_copy(part, part, sem)

    turn_in(0)
    turn_in(1)
    pl.semaphore_wait(barrier, len(near))
    for device, dz in above:
        pl.semaphore_signal(ready.at[4 - dz], inc=1, device_id=device, device_id_type=MESH)
    each_peer(lambda device, d: copy_target(device, d).start(), ((0,),))
    for steps in ((1, 3), (2,)):
        for dz in steps:
            pl.semaphore_wait(ready.at[dz], 1)
        each_peer(lambda device, d: copy_target(device, d).start(), (steps,))
        each_peer(lambda device, d: copy_in(0, device, d).start(), (steps,))
    each_peer(lambda device, d: copy_in(0, device, d).start(), ((0,),))
    each_peer(lambda device, d: copy_in(1, device, d).start(), IN_TURN)
    for q in range(CHUNKS):
        recv[q][own, :] = send[home(q, me), :]
    trecv[me] = tsend[me // 8]

    small[1].wait()
    small[2].wait()
    for k in range(9):
        level, s = divmod(k, 3)
        for c in range(2):
            re = interp_ref[level, s, c, 0]
            im = interp_ref[level, s, c, 1]
            wide[0:64, 0:64] = re
            wide[0:64, 64:128] = -im
            wide[64:128, 0:64] = im
            wide[64:128, 64:128] = re
            w = wide[...].T
            hi = w.astype(jnp.bfloat16)
            lo = (w - hi.astype(jnp.float32)).astype(jnp.bfloat16)
            rows = slice(c * 128, (c + 1) * 128)
            weights[k, rows, 0:128] = hi
            weights[k, rows, 128:256] = lo
    for level in range(3):
        for s in range(3):
            f = freq_ref[level, s].astype(jnp.float32) * (1.0 / 1024.0)
            k = (level * 3 + s) * 2
            freqs[k : k + 2, 0:64] = f
            freqs[k : k + 2, 64:128] = f

    lane = lax.broadcasted_iota(jnp.int32, (8, 128), 1)
    row = lax.broadcasted_iota(jnp.int32, (8, 128), 0)
    all_targets(trecv_sem).wait()
    for q in range(CHUNKS):

        mine = lane == (me % 8) * (CHUNKS * ROWS) + q * ROWS + row

        def gather(i, carry, q=q, mine=mine):
            t = trecv[i]
            t = jnp.sum(jnp.where(mine, t, 0.0), axis=1, keepdims=True)
            turns[pl.ds(pl.multiple_of(q * half + i * 8, 8), 8), :] = jnp.broadcast_to(t, (8, 128))
            return carry

        lax.fori_loop(0, GROUP, gather, 0, unroll=8)

    lane1 = lax.broadcasted_iota(jnp.int32, (1, 128), 1)
    quarter = jnp.where(lane1 < 64, 0.0, -0.25)

    def fill(q, first, last):
        def body(i, carry):
            rows = pl.ds(pl.multiple_of(q * half + i * 64, 64), 64)
            t = turns[rows, :]
            low_half = lax.broadcasted_iota(jnp.int32, t.shape, 1) < 64
            for k in range(18):
                p = turn_cos(t * freqs[k : k + 1, :] + quarter)
                other = pltpu.roll(p, 64, 1)
                cosines[k, rows, :] = jnp.where(low_half, p, other)
                sines[k, rows, :] = jnp.where(low_half, -other, p)
            return carry

        lax.fori_loop(first, last, body, 0)

    def mix(k, rows, child0, child1):
        rot = []
        for c, x in enumerate((child0, child1)):
            rot.append(cosines[2 * k + c, rows, :] * x + sines[2 * k + c, rows, :] * pltpu.roll(x, 64, 1))
        rot = jnp.concatenate(rot, axis=1)
        hi = rot.astype(jnp.bfloat16)
        lo = (rot - hi.astype(jnp.float32)).astype(jnp.bfloat16)
        both = jnp.dot(hi, weights[k], preferred_element_type=jnp.float32)
        rest = jnp.dot(lo, weights[k, :, 0:128], preferred_element_type=jnp.float32)
        return both[:, 0:128] + both[:, 128:256] + rest

    def step(k, q, src, dst):
        stride = ROWS << STEP_BITS[k]
        base = q * half
        if stride >= BLOCK:
            for at in range(0, half, BLOCK):
                if at & stride == 0:
                    x0 = src[at : at + BLOCK, :]
                    x1 = src[at + stride : at + stride + BLOCK, :]
                    for here in (at, at + stride):
                        dst[here : here + BLOCK, :] = mix(
                            k, slice(base + here, base + here + BLOCK), x0, x1
                        )
        else:
            for at in range(0, half, BLOCK):
                x = src[at : at + BLOCK, :].reshape(BLOCK // (2 * stride), 2, stride, 128)
                children = [
                    jnp.broadcast_to(x[:, c : c + 1], x.shape).reshape(BLOCK, 128) for c in range(2)
                ]
                dst[at : at + BLOCK, :] = mix(k, slice(base + at, base + at + BLOCK), *children)

    fill(0, 0, half // 64)
    for q in range(CHUNKS):
        all_of(recv[q], in_recv.at[q]).wait()
        states = [recv[q]] + [(state0, state1)[k % 2] for k in range(8)] + [back[q]]
        for k in range(9):
            step(k, q, states[k], states[k + 1])
        each_peer(
            lambda device, d, q=q: copy_out(q, device, d).start(), AWAY_FIRST if q else IN_TURN
        )
        keep(q).start()
        if q == 0:
            fill(1, 0, half // 64)

    for q in range(CHUNKS):
        all_of(rows_ref, out_recv.at[q]).wait()
        keep(q).wait()
    all_targets(tsend_sem).wait()
    for q in range(CHUNKS):
        all_of(send, in_send.at[q]).wait()
        all_of(back[q], out_send.at[q]).wait()


def turn_kernel(rows_ref, out_ref, y_ref, sem):
    copies = []
    for i in range(rows_ref.shape[0] // TURN):
        for j in range(i * TURN, (i + 1) * TURN, 128):
            y_ref[:, :, j : j + 128] = rows_ref[j : j + 128, :].T.reshape(2, 64, 128)
        cols = pl.ds(i * TURN, TURN)
        copies.append(pltpu.make_async_copy(y_ref.at[:, :, cols], out_ref.at[:, :, cols], sem.at[i]))
        copies[i].start()
    for copy in copies:
        copy.wait()


def shards(coeffs, interp, freq_index, target):
    f32 = jnp.float32
    anywhere = pl.BlockSpec(memory_space=pl.ANY)
    big = pltpu.VMEM((CHUNK, 128), f32)
    dma = pltpu.SemaphoreType.DMA
    positions = coeffs.shape[2]
    rows = pl.pallas_call(
        kernel,
        out_shape=jax.ShapeDtypeStruct((positions, 128), f32),
        in_specs=[pl.BlockSpec(memory_space=pltpu.HBM)] * 4,
        out_specs=anywhere,
        scratch_shapes=[
            pltpu.VMEM(coeffs.shape, f32),
            pltpu.VMEM((CHUNKS * CHUNK, 128), f32),
            big, big, big, big, big, big,
            pltpu.VMEM(interp.shape, f32),
            pltpu.VMEM(freq_index.shape, jnp.int32),
            pltpu.VMEM((16, 128), jnp.int32),
            pltpu.VMEM((16, 1, 128), f32),
            pltpu.VMEM((GROUP, 1, 128), f32),
            pltpu.VMEM((CHUNKS * CHUNK, 128), f32),
            pltpu.VMEM((24, 128), f32),
            pltpu.VMEM((128, 128), f32),
            pltpu.VMEM((9, 256, 256), jnp.bfloat16),
            pltpu.VMEM((18, CHUNKS * CHUNK, 128), f32),
            pltpu.VMEM((18, CHUNKS * CHUNK, 128), f32),
            pltpu.SemaphoreType.REGULAR((4,)),
            dma((CHUNKS,)), dma((3,)), dma((CHUNKS,)), dma, dma,
            dma((CHUNKS,)), dma((CHUNKS,)), dma((CHUNKS,)), dma((CHUNKS,)),
        ],
        compiler_params=pltpu.CompilerParams(
            collective_id=0, has_side_effects=True, vmem_limit_bytes=52 * 1024 * 1024
        ),
        name="butterfly",
    )(*(
        pltpu.with_memory_space_constraint(x, pltpu.HBM)
        for x in (coeffs, interp, freq_index, target.reshape(16, 128))
    ))
    rows = pltpu.with_memory_space_constraint(rows, pltpu.VMEM)
    return pl.pallas_call(
        turn_kernel,
        out_shape=jax.ShapeDtypeStruct(coeffs.shape, f32),
        in_specs=[pl.BlockSpec(memory_space=pltpu.VMEM)],
        out_specs=pl.BlockSpec(memory_space=pltpu.HBM),
        scratch_shapes=[pltpu.VMEM(coeffs.shape, f32), dma((positions // TURN,))],
        name="turn",
    )(rows)


def solution(mesh):
    in_specs = (P(None, None, ("gx", "gy", "gz")), P(), P(), P(("gx", "gy", "gz")))
    out_specs = P(None, None, ("gx", "gy", "gz"))
    return jax.shard_map(shards, mesh=mesh, in_specs=in_specs, out_specs=out_specs, check_vma=False)
```

```python
import functools
import math

import jax
import jax.numpy as jnp
import numpy as np
from jax import lax
from jax.experimental import pallas as pl
from jax.experimental.pallas import tpu as pltpu
from jax.sharding import PartitionSpec as P

MESH = pl.DeviceIdType.MESH
GROUP = 128
PEERS = GROUP - 1
CHUNKS = 2
ROWS = 8
CHUNK = GROUP * ROWS
STEP_BITS = (6, 2, 0, 5, 3, 1, 4, 2, 0)
BLOCK = 256
TURN = 512


def turn_cos_coefficients(degree=6):
    nodes = np.cos((np.arange(400) + 0.5) * np.pi / 400)
    z = (nodes + 1) / 8
    cheb = np.polynomial.chebyshev.Chebyshev.fit(
        z, np.cos(2 * np.pi * np.sqrt(z)), degree, domain=[0, 0.25]
    )
    poly = cheb.convert(kind=np.polynomial.Polynomial, domain=[-1, 1], window=[-1, 1])
    return [float(c) for c in poly.coef]


COS = turn_cos_coefficients()


def turn_cos(r):
    x = r - jnp.round(r)
    z = x * x
    acc = jnp.full_like(z, COS[-1])
    for c in COS[-2::-1]:
        acc = acc * z + c
    return acc


def place():
    gx, gy, gz = lax.axis_index("gx"), lax.axis_index("gy"), lax.axis_index("gz")
    return gx // 8, (gx // 2) % 4, gy, gz, gx % 2


def number(xlo, z, y, g):
    return ((xlo * 4 + z) * 4 + y) * 4 + g


AWAY_FIRST = ((2,), (1, 3), (0,))
IN_TURN = ((2, 1, 0, 3),)


def each_peer(fn, order=AWAY_FIRST, turns=(0, 1, 2, 3)):
    xlo, z, y, g, low = place()
    xs = [(xlo + i) % 2 for i in range(2)]
    zs = [(z + i) % 4 for i in range(4)]
    ys = [(y + i) % 4 for i in range(4)]
    gs = [(g + i) % 4 for i in range(4)]
    for dzs in order:
        for dx in range(2):
            for dy in range(4):
                for dg in turns:
                    for dz in dzs:
                        if dz or dx or dy or dg:
                            gx = xs[dx] * 8 + zs[dz] * 2 + low
                            first = number(xs[dx], zs[dz], 0, 0)
                            fn((gx, ys[dy], gs[dg]), first + ys[dy] * 4 + gs[dg])


def kernel(
    coeffs_ref, interp_hbm, freq_hbm, target_hbm, rows_ref,
    x_ref, send, recv0, recv1, state0, state1, back0, back1,
    interp_ref, freq_ref, target_ref,
    tsend, trecv, turns, freqs, wide, weights, cosines, sines,
    sibling_sem, load_sem, small_sem, own_sem, tsend_sem, trecv_sem, in_send, in_recv, out_send, out_recv,
):
    xlo, z, y, g, low = place()
    me = number(xlo, z, y, g)
    core = g % 2
    recv, back = (recv0, recv1), (back0, back1)
    own = pl.ds(pl.multiple_of(me * ROWS, ROWS), ROWS)
    half = CHUNK

    def home(q, d):
        return pl.ds(pl.multiple_of((d * CHUNKS + q) * ROWS, ROWS), ROWS)

    def load(q):
        cols = pl.ds(q * half, half)
        return pltpu.make_async_copy(
            coeffs_ref.at[:, :, cols], x_ref.at[:, :, cols], load_sem.at[q]
        )

    barrier = pltpu.get_barrier_semaphore()
    each_peer(
        lambda device, d: pl.semaphore_signal(
            barrier, inc=1, device_id=device, device_id_type=MESH
        )
    )

    small = [
        pltpu.make_async_copy(src, dst, small_sem.at[i])
        for i, (src, dst) in enumerate(
            ((target_hbm, target_ref), (freq_hbm, freq_ref), (interp_hbm, interp_ref))
        )
    ]
    small[0].start()
    for q in range(CHUNKS):
        load(q).start()
    small[1].start()
    small[2].start()

    small[0].wait()
    targets = target_ref[...].astype(jnp.float32)
    for k in range(16):
        tsend[k] = targets[k : k + 1, :]

    def turn_in(q):
        load(q).wait()
        for j in range(half // 128):
            cols = slice(q * half + j * 128, q * half + (j + 1) * 128)
            block = x_ref[:, :, cols].reshape(128, 128)
            send[q * half + j * 128 : q * half + (j + 1) * 128, :] = block.T

    def copy_in(q, device, d):
        return pltpu.make_async_remote_copy(
            src_ref=send.at[home(q, d)],
            dst_ref=recv[q].at[pl.ds(pl.multiple_of(me * ROWS, ROWS), ROWS)],
            send_sem=in_send.at[q],
            recv_sem=in_recv.at[q],
            device_id=device,
            device_id_type=MESH,
        )

    def copy_out(q, device, d):
        return pltpu.make_async_remote_copy(
            src_ref=back[q].at[pl.ds(pl.multiple_of(d * ROWS, ROWS), ROWS)],
            dst_ref=rows_ref.at[home(q, me)],
            send_sem=out_send.at[q],
            recv_sem=out_recv.at[q],
            device_id=device,
            device_id_type=MESH,
        )

    def copy_target(device, d):
        return pltpu.make_async_remote_copy(
            src_ref=tsend.at[d // 8],
            dst_ref=trecv.at[core, me // 2],
            send_sem=tsend_sem,
            recv_sem=trecv_sem,
            device_id=device,
            device_id_type=MESH,
        )

    def keep(q):
        return pltpu.make_async_copy(
            back[q].at[own],
            rows_ref.at[home(q, me)],
            own_sem.at[q],
        )

    def all_of(ref, sem):
        part = ref.at[pl.ds(0, PEERS * ROWS)]
        return pltpu.make_async_copy(part, part, sem)

    def all_targets(sem):
        part = trecv.at[0, pl.ds(0, GROUP // 2 - 1)]
        return pltpu.make_async_copy(part, part, sem)

    def own_target():
        return pltpu.make_async_copy(tsend.at[me // 8], trecv.at[core, me // 2], sibling_sem.at[0])

    def to_sibling(part):
        return pltpu.make_async_remote_copy(
            src_ref=trecv.at[part],
            dst_ref=trecv.at[part],
            send_sem=sibling_sem.at[1],
            recv_sem=sibling_sem.at[2],
            device_id=(lax.axis_index("gx"), y, g + 1 - 2 * core),
            device_id_type=MESH,
        )

    turn_in(0)
    turn_in(1)
    pl.semaphore_wait(barrier, PEERS)
    each_peer(lambda device, d: copy_target(device, d).start(), turns=(0, 2))
    own_target().start()
    each_peer(lambda device, d: copy_in(0, device, d).start(), IN_TURN)
    each_peer(lambda device, d: copy_in(1, device, d).start(), IN_TURN)
    for q in range(CHUNKS):
        recv[q][own, :] = send[home(q, me), :]

    small[1].wait()
    small[2].wait()
    for k in range(9):
        level, s = divmod(k, 3)
        for c in range(2):
            re = interp_ref[level, s, c, 0]
            im = interp_ref[level, s, c, 1]
            wide[0:64, 0:64] = re
            wide[0:64, 64:128] = -im
            wide[64:128, 0:64] = im
            wide[64:128, 64:128] = re
            w = wide[...].T
            hi = w.astype(jnp.bfloat16)
            lo = (w - hi.astype(jnp.float32)).astype(jnp.bfloat16)
            rows = slice(c * 128, (c + 1) * 128)
            weights[k, rows, 0:128] = hi
            weights[k, rows, 128:256] = lo
    for level in range(3):
        for s in range(3):
            f = freq_ref[level, s].astype(jnp.float32) * (1.0 / 1024.0)
            k = (level * 3 + s) * 2
            freqs[k : k + 2, 0:64] = f
            freqs[k : k + 2, 64:128] = f

    lane = lax.broadcasted_iota(jnp.int32, (8, 128), 1)
    row = lax.broadcasted_iota(jnp.int32, (8, 128), 0)
    all_targets(trecv_sem).wait()
    own_target().wait()
    to_sibling(core).start()
    to_sibling(1 - core).wait_recv()
    for q in range(CHUNKS):

        mine = lane == (me % 8) * (CHUNKS * ROWS) + q * ROWS + row

        def gather(i, carry, q=q, mine=mine):
            t = trecv[i % 2, i // 2]
            t = jnp.sum(jnp.where(mine, t, 0.0), axis=1, keepdims=True)
            turns[pl.ds(pl.multiple_of(q * half + i * 8, 8), 8), :] = jnp.broadcast_to(t, (8, 128))
            return carry

        lax.fori_loop(0, GROUP, gather, 0, unroll=8)

    lane1 = lax.broadcasted_iota(jnp.int32, (1, 128), 1)
    quarter = jnp.where(lane1 < 64, 0.0, -0.25)

    def fill(q, first, last):
        def body(i, carry):
            rows = pl.ds(pl.multiple_of(q * half + i * 64, 64), 64)
            t = turns[rows, :]
            low_half = lax.broadcasted_iota(jnp.int32, t.shape, 1) < 64
            for k in range(18):
                p = turn_cos(t * freqs[k : k + 1, :] + quarter)
                other = pltpu.roll(p, 64, 1)
                cosines[k, rows, :] = jnp.where(low_half, p, other)
                sines[k, rows, :] = jnp.where(low_half, -other, p)
            return carry

        lax.fori_loop(first, last, body, 0)

    def mix(k, rows, child0, child1):
        rot = []
        for c, x in enumerate((child0, child1)):
            rot.append(cosines[2 * k + c, rows, :] * x + sines[2 * k + c, rows, :] * pltpu.roll(x, 64, 1))
        rot = jnp.concatenate(rot, axis=1)
        hi = rot.astype(jnp.bfloat16)
        lo = (rot - hi.astype(jnp.float32)).astype(jnp.bfloat16)
        both = jnp.dot(hi, weights[k], preferred_element_type=jnp.float32)
        rest = jnp.dot(lo, weights[k, :, 0:128], preferred_element_type=jnp.float32)
        return both[:, 0:128] + both[:, 128:256] + rest

    def step(k, q, src, dst):
        stride = ROWS << STEP_BITS[k]
        base = q * half
        if stride >= BLOCK:
            for at in range(0, half, BLOCK):
                if at & stride == 0:
                    x0 = src[at : at + BLOCK, :]
                    x1 = src[at + stride : at + stride + BLOCK, :]
                    for here in (at, at + stride):
                        dst[here : here + BLOCK, :] = mix(
                            k, slice(base + here, base + here + BLOCK), x0, x1
                        )
        else:
            for at in range(0, half, BLOCK):
                x = src[at : at + BLOCK, :].reshape(BLOCK // (2 * stride), 2, stride, 128)
                children = [
                    jnp.broadcast_to(x[:, c : c + 1], x.shape).reshape(BLOCK, 128) for c in range(2)
                ]
                dst[at : at + BLOCK, :] = mix(k, slice(base + at, base + at + BLOCK), *children)

    fill(0, 0, half // 64)
    for q in range(CHUNKS):
        all_of(recv[q], in_recv.at[q]).wait()
        states = [recv[q]] + [(state0, state1)[k % 2] for k in range(8)] + [back[q]]
        for k in range(9):
            step(k, q, states[k], states[k + 1])
        each_peer(
            lambda device, d, q=q: copy_out(q, device, d).start(), AWAY_FIRST if q else IN_TURN
        )
        keep(q).start()
        if q == 0:
            fill(1, 0, half // 64)

    for q in range(CHUNKS):
        all_of(rows_ref, out_recv.at[q]).wait()
        keep(q).wait()
    all_targets(tsend_sem).wait()
    to_sibling(core).wait_send()
    for q in range(CHUNKS):
        all_of(send, in_send.at[q]).wait()
        all_of(back[q], out_send.at[q]).wait()


def turn_kernel(rows_ref, out_ref, y_ref, sem):
    copies = []
    for i in range(rows_ref.shape[0] // TURN):
        for j in range(i * TURN, (i + 1) * TURN, 128):
            y_ref[:, :, j : j + 128] = rows_ref[j : j + 128, :].T.reshape(2, 64, 128)
        cols = pl.ds(i * TURN, TURN)
        copies.append(pltpu.make_async_copy(y_ref.at[:, :, cols], out_ref.at[:, :, cols], sem.at[i]))
        copies[i].start()
    for copy in copies:
        copy.wait()


def shards(coeffs, interp, freq_index, target):
    f32 = jnp.float32
    anywhere = pl.BlockSpec(memory_space=pl.ANY)
    big = pltpu.VMEM((CHUNK, 128), f32)
    dma = pltpu.SemaphoreType.DMA
    positions = coeffs.shape[2]
    rows = pl.pallas_call(
        kernel,
        out_shape=jax.ShapeDtypeStruct((positions, 128), f32),
        in_specs=[pl.BlockSpec(memory_space=pltpu.HBM)] * 4,
        out_specs=anywhere,
        scratch_shapes=[
            pltpu.VMEM(coeffs.shape, f32),
            pltpu.VMEM((CHUNKS * CHUNK, 128), f32),
            big, big, big, big, big, big,
            pltpu.VMEM(interp.shape, f32),
            pltpu.VMEM(freq_index.shape, jnp.int32),
            pltpu.VMEM((16, 128), jnp.int32),
            pltpu.VMEM((16, 1, 128), f32),
            pltpu.VMEM((2, GROUP // 2, 1, 128), f32),
            pltpu.VMEM((CHUNKS * CHUNK, 128), f32),
            pltpu.VMEM((24, 128), f32),
            pltpu.VMEM((128, 128), f32),
            pltpu.VMEM((9, 256, 256), jnp.bfloat16),
            pltpu.VMEM((18, CHUNKS * CHUNK, 128), f32),
            pltpu.VMEM((18, CHUNKS * CHUNK, 128), f32),
            dma((3,)),
            dma((CHUNKS,)), dma((3,)), dma((CHUNKS,)), dma, dma,
            dma((CHUNKS,)), dma((CHUNKS,)), dma((CHUNKS,)), dma((CHUNKS,)),
        ],
        compiler_params=pltpu.CompilerParams(
            collective_id=0, has_side_effects=True, vmem_limit_bytes=52 * 1024 * 1024
        ),
        name="butterfly",
    )(*(
        pltpu.with_memory_space_constraint(x, pltpu.HBM)
        for x in (coeffs, interp, freq_index, target.reshape(16, 128))
    ))
    rows = pltpu.with_memory_space_constraint(rows, pltpu.VMEM)
    return pl.pallas_call(
        turn_kernel,
        out_shape=jax.ShapeDtypeStruct(coeffs.shape, f32),
        in_specs=[pl.BlockSpec(memory_space=pltpu.VMEM)],
        out_specs=pl.BlockSpec(memory_space=pltpu.HBM),
        scratch_shapes=[pltpu.VMEM(coeffs.shape, f32), dma((positions // TURN,))],
        name="turn",
    )(rows)


def solution(mesh):
    in_specs = (P(None, None, ("gx", "gy", "gz")), P(), P(), P(("gx", "gy", "gz")))
    out_specs = P(None, None, ("gx", "gy", "gz"))
    return jax.shard_map(shards, mesh=mesh, in_specs=in_specs, out_specs=out_specs, check_vma=False)
```

```python
import functools
import math

import jax
import jax.numpy as jnp
import numpy as np
from jax import lax
from jax.experimental import pallas as pl
from jax.experimental.pallas import tpu as pltpu
from jax.sharding import PartitionSpec as P

MESH = pl.DeviceIdType.MESH
GROUP = 128
PEERS = GROUP - 1
CHUNKS = 2
ROWS = 8
CHUNK = GROUP * ROWS
STEP_BITS = (6, 2, 0, 5, 3, 1, 4, 2, 0)
BLOCK = 256
TURN = 512


def turn_cos_coefficients(degree=6):
    nodes = np.cos((np.arange(400) + 0.5) * np.pi / 400)
    z = (nodes + 1) / 8
    cheb = np.polynomial.chebyshev.Chebyshev.fit(
        z, np.cos(2 * np.pi * np.sqrt(z)), degree, domain=[0, 0.25]
    )
    poly = cheb.convert(kind=np.polynomial.Polynomial, domain=[-1, 1], window=[-1, 1])
    return [float(c) for c in poly.coef]


COS = turn_cos_coefficients()


def turn_cos(r):
    x = r - jnp.round(r)
    z = x * x
    acc = jnp.full_like(z, COS[-1])
    for c in COS[-2::-1]:
        acc = acc * z + c
    return acc


def place():
    gx, gy, gz = lax.axis_index("gx"), lax.axis_index("gy"), lax.axis_index("gz")
    return gx // 8, (gx // 2) % 4, gy, gz, gx % 2


def number(xlo, z, y, g):
    return ((xlo * 4 + z) * 4 + y) * 4 + g


AWAY_FIRST = ((2,), (1, 3), (0,))
IN_TURN = ((2, 1, 0, 3),)


def each_peer(fn, order=AWAY_FIRST, turns=(0, 1, 2, 3)):
    xlo, z, y, g, low = place()
    xs = [(xlo + i) % 2 for i in range(2)]
    zs = [(z + i) % 4 for i in range(4)]
    ys = [(y + i) % 4 for i in range(4)]
    gs = [(g + i) % 4 for i in range(4)]
    for dzs in order:
        for dx in range(2):
            for dy in range(4):
                for dg in turns:
                    for dz in dzs:
                        if dz or dx or dy or dg:
                            gx = xs[dx] * 8 + zs[dz] * 2 + low
                            first = number(xs[dx], zs[dz], 0, 0)
                            fn((gx, ys[dy], gs[dg]), first + ys[dy] * 4 + gs[dg])


def kernel(
    coeffs_ref, interp_hbm, freq_hbm, target_hbm, rows_ref,
    x_ref, send, recv0, recv1, state0, state1, back0, back1,
    interp_ref, freq_ref, target_ref,
    tsend, trecv, turns, freqs, wide, weights, cosines, sines,
    sibling_sem, load_sem, small_sem, own_sem, tsend_sem, trecv_sem, in_send, in_recv, out_send, out_recv,
):
    xlo, z, y, g, low = place()
    me = number(xlo, z, y, g)
    core = g % 2
    recv, back = (recv0, recv1), (back0, back1)
    own = pl.ds(pl.multiple_of(me * ROWS, ROWS), ROWS)
    half = CHUNK

    def home(q, d):
        return pl.ds(pl.multiple_of((d * CHUNKS + q) * ROWS, ROWS), ROWS)

    def load(q):
        cols = pl.ds(q * half, half)
        return pltpu.make_async_copy(
            coeffs_ref.at[:, :, cols], x_ref.at[:, :, cols], load_sem.at[q]
        )

    barrier = pltpu.get_barrier_semaphore()
    each_peer(
        lambda device, d: pl.semaphore_signal(
            barrier, inc=1, device_id=device, device_id_type=MESH
        )
    )

    small = [
        pltpu.make_async_copy(src, dst, small_sem.at[i])
        for i, (src, dst) in enumerate(
            ((target_hbm, target_ref), (freq_hbm, freq_ref), (interp_hbm, interp_ref))
        )
    ]
    small[0].start()
    for q in range(CHUNKS):
        load(q).start()
    small[1].start()
    small[2].start()

    small[0].wait()
    targets = target_ref[...].astype(jnp.float32)
    for k in range(16):
        tsend[k] = targets[k : k + 1, :]

    def turn_in(q):
        load(q).wait()
        for j in range(half // 128):
            cols = slice(q * half + j * 128, q * half + (j + 1) * 128)
            block = x_ref[:, :, cols].reshape(128, 128)
            send[q * half + j * 128 : q * half + (j + 1) * 128, :] = block.T

    def copy_in(q, device, d):
        return pltpu.make_async_remote_copy(
            src_ref=send.at[home(q, d)],
            dst_ref=recv[q].at[pl.ds(pl.multiple_of(me * ROWS, ROWS), ROWS)],
            send_sem=in_send.at[q],
            recv_sem=in_recv.at[q],
            device_id=device,
            device_id_type=MESH,
        )

    def copy_out(q, device, d):
        return pltpu.make_async_remote_copy(
            src_ref=back[q].at[pl.ds(pl.multiple_of(d * ROWS, ROWS), ROWS)],
            dst_ref=rows_ref.at[home(q, me)],
            send_sem=out_send.at[q],
            recv_sem=out_recv.at[q],
            device_id=device,
            device_id_type=MESH,
        )

    def copy_target(device, d):
        return pltpu.make_async_remote_copy(
            src_ref=tsend.at[d // 8],
            dst_ref=trecv.at[core, me // 2],
            send_sem=tsend_sem,
            recv_sem=trecv_sem,
            device_id=device,
            device_id_type=MESH,
        )

    def keep(q):
        return pltpu.make_async_copy(
            back[q].at[own],
            rows_ref.at[home(q, me)],
            own_sem.at[q],
        )

    def all_of(ref, sem):
        part = ref.at[pl.ds(0, PEERS * ROWS)]
        return pltpu.make_async_copy(part, part, sem)

    def all_targets(sem):
        part = trecv.at[0, pl.ds(0, GROUP // 2 - 1)]
        return pltpu.make_async_copy(part, part, sem)

    def own_target():
        return pltpu.make_async_copy(tsend.at[me // 8], trecv.at[core, me // 2], sibling_sem.at[0])

    def to_sibling(part):
        return pltpu.make_async_remote_copy(
            src_ref=trecv.at[part],
            dst_ref=trecv.at[part],
            send_sem=sibling_sem.at[1],
            recv_sem=sibling_sem.at[2],
            device_id=(lax.axis_index("gx"), y, g + 1 - 2 * core),
            device_id_type=MESH,
        )

    turn_in(0)
    turn_in(1)
    pl.semaphore_wait(barrier, PEERS)
    each_peer(lambda device, d: copy_target(device, d).start(), turns=(0, 2))
    own_target().start()
    each_peer(lambda device, d: copy_in(0, device, d).start(), IN_TURN)
    each_peer(lambda device, d: copy_in(1, device, d).start(), IN_TURN)
    for q in range(CHUNKS):
        recv[q][own, :] = send[home(q, me), :]

    small[1].wait()
    small[2].wait()
    for k in range(9):
        level, s = divmod(k, 3)
        for c in range(2):
            re = interp_ref[level, s, c, 0]
            im = interp_ref[level, s, c, 1]
            wide[0:64, 0:64] = re
            wide[0:64, 64:128] = -im
            wide[64:128, 0:64] = im
            wide[64:128, 64:128] = re
            w = wide[...].T
            hi = w.astype(jnp.bfloat16)
            lo = (w - hi.astype(jnp.float32)).astype(jnp.bfloat16)
            rows = slice(c * 128, (c + 1) * 128)
            weights[k, rows, 0:128] = hi
            weights[k, rows, 128:256] = lo
    for level in range(3):
        for s in range(3):
            f = freq_ref[level, s].astype(jnp.float32) * (1.0 / 1024.0)
            k = (level * 3 + s) * 2
            freqs[k : k + 2, 0:64] = f
            freqs[k : k + 2, 64:128] = f

    lane = lax.broadcasted_iota(jnp.int32, (8, 128), 1)
    row = lax.broadcasted_iota(jnp.int32, (8, 128), 0)
    all_targets(trecv_sem).wait()
    own_target().wait()
    to_sibling(core).start()
    to_sibling(1 - core).wait_recv()
    def gather(q):
        mine = lane == (me % 8) * (CHUNKS * ROWS) + q * ROWS + row

        def body(i, carry):
            t = jnp.sum(jnp.where(mine, trecv[i % 2, i // 2], 0.0), axis=1, keepdims=True)
            turns[pl.ds(pl.multiple_of(q * half + i * 8, 8), 8), :] = jnp.broadcast_to(t, (8, 128))
            return carry

        lax.fori_loop(0, GROUP, body, 0, unroll=8)

    gather(0)
    lane1 = lax.broadcasted_iota(jnp.int32, (1, 128), 1)
    quarter = jnp.where(lane1 < 64, 0.0, -0.25)

    def fill(q, first, last):
        def body(i, carry):
            rows = pl.ds(pl.multiple_of(q * half + i * 64, 64), 64)
            t = turns[rows, :]
            low_half = lax.broadcasted_iota(jnp.int32, t.shape, 1) < 64
            for k in range(18):
                p = turn_cos(t * freqs[k : k + 1, :] + quarter)
                other = pltpu.roll(p, 64, 1)
                cosines[k, rows, :] = jnp.where(low_half, p, other)
                sines[k, rows, :] = jnp.where(low_half, -other, p)
            return carry

        lax.fori_loop(first, last, body, 0)

    def mix(k, rows, child0, child1):
        rot = []
        for c, x in enumerate((child0, child1)):
            rot.append(cosines[2 * k + c, rows, :] * x + sines[2 * k + c, rows, :] * pltpu.roll(x, 64, 1))
        rot = jnp.concatenate(rot, axis=1)
        hi = rot.astype(jnp.bfloat16)
        lo = (rot - hi.astype(jnp.float32)).astype(jnp.bfloat16)
        both = jnp.dot(hi, weights[k], preferred_element_type=jnp.float32)
        rest = jnp.dot(lo, weights[k, :, 0:128], preferred_element_type=jnp.float32)
        return both[:, 0:128] + both[:, 128:256] + rest

    def step(k, q, src, dst):
        stride = ROWS << STEP_BITS[k]
        base = q * half
        if stride >= BLOCK:
            for at in range(0, half, BLOCK):
                if at & stride == 0:
                    x0 = src[at : at + BLOCK, :]
                    x1 = src[at + stride : at + stride + BLOCK, :]
                    for here in (at, at + stride):
                        dst[here : here + BLOCK, :] = mix(
                            k, slice(base + here, base + here + BLOCK), x0, x1
                        )
        else:
            for at in range(0, half, BLOCK):
                x = src[at : at + BLOCK, :].reshape(BLOCK // (2 * stride), 2, stride, 128)
                children = [
                    jnp.broadcast_to(x[:, c : c + 1], x.shape).reshape(BLOCK, 128) for c in range(2)
                ]
                dst[at : at + BLOCK, :] = mix(k, slice(base + at, base + at + BLOCK), *children)

    fill(0, 0, half // 64)
    for q in range(CHUNKS):
        all_of(recv[q], in_recv.at[q]).wait()
        states = [recv[q]] + [(state0, state1)[k % 2] for k in range(8)] + [back[q]]
        for k in range(9):
            step(k, q, states[k], states[k + 1])
        each_peer(
            lambda device, d, q=q: copy_out(q, device, d).start(), AWAY_FIRST if q else IN_TURN
        )
        keep(q).start()
        if q == 0:
            gather(1)
            fill(1, 0, half // 64)

    for q in range(CHUNKS):
        all_of(rows_ref, out_recv.at[q]).wait()
        keep(q).wait()
    all_targets(tsend_sem).wait()
    to_sibling(core).wait_send()
    for q in range(CHUNKS):
        all_of(send, in_send.at[q]).wait()
        all_of(back[q], out_send.at[q]).wait()


def turn_kernel(rows_ref, out_ref, y_ref, sem):
    copies = []
    for i in range(rows_ref.shape[0] // TURN):
        for j in range(i * TURN, (i + 1) * TURN, 128):
            y_ref[:, :, j : j + 128] = rows_ref[j : j + 128, :].T.reshape(2, 64, 128)
        cols = pl.ds(i * TURN, TURN)
        copies.append(pltpu.make_async_copy(y_ref.at[:, :, cols], out_ref.at[:, :, cols], sem.at[i]))
        copies[i].start()
    for copy in copies:
        copy.wait()


def shards(coeffs, interp, freq_index, target):
    f32 = jnp.float32
    anywhere = pl.BlockSpec(memory_space=pl.ANY)
    big = pltpu.VMEM((CHUNK, 128), f32)
    dma = pltpu.SemaphoreType.DMA
    positions = coeffs.shape[2]
    rows = pl.pallas_call(
        kernel,
        out_shape=jax.ShapeDtypeStruct((positions, 128), f32),
        in_specs=[pl.BlockSpec(memory_space=pltpu.HBM)] * 4,
        out_specs=anywhere,
        scratch_shapes=[
            pltpu.VMEM(coeffs.shape, f32),
            pltpu.VMEM((CHUNKS * CHUNK, 128), f32),
            big, big, big, big, big, big,
            pltpu.VMEM(interp.shape, f32),
            pltpu.VMEM(freq_index.shape, jnp.int32),
            pltpu.VMEM((16, 128), jnp.int32),
            pltpu.VMEM((16, 1, 128), f32),
            pltpu.VMEM((2, GROUP // 2, 1, 128), f32),
            pltpu.VMEM((CHUNKS * CHUNK, 128), f32),
            pltpu.VMEM((24, 128), f32),
            pltpu.VMEM((128, 128), f32),
            pltpu.VMEM((9, 256, 256), jnp.bfloat16),
            pltpu.VMEM((18, CHUNKS * CHUNK, 128), f32),
            pltpu.VMEM((18, CHUNKS * CHUNK, 128), f32),
            dma((3,)),
            dma((CHUNKS,)), dma((3,)), dma((CHUNKS,)), dma, dma,
            dma((CHUNKS,)), dma((CHUNKS,)), dma((CHUNKS,)), dma((CHUNKS,)),
        ],
        compiler_params=pltpu.CompilerParams(
            collective_id=0, has_side_effects=True, vmem_limit_bytes=52 * 1024 * 1024
        ),
        name="butterfly",
    )(*(
        pltpu.with_memory_space_constraint(x, pltpu.HBM)
        for x in (coeffs, interp, freq_index, target.reshape(16, 128))
    ))
    rows = pltpu.with_memory_space_constraint(rows, pltpu.VMEM)
    return pl.pallas_call(
        turn_kernel,
        out_shape=jax.ShapeDtypeStruct(coeffs.shape, f32),
        in_specs=[pl.BlockSpec(memory_space=pltpu.VMEM)],
        out_specs=pl.BlockSpec(memory_space=pltpu.HBM),
        scratch_shapes=[pltpu.VMEM(coeffs.shape, f32), dma((positions // TURN,))],
        name="turn",
    )(rows)


def solution(mesh):
    in_specs = (P(None, None, ("gx", "gy", "gz")), P(), P(), P(("gx", "gy", "gz")))
    out_specs = P(None, None, ("gx", "gy", "gz"))
    return jax.shard_map(shards, mesh=mesh, in_specs=in_specs, out_specs=out_specs, check_vma=False)
```
